32 devices in a mesh: dp: 8 (over z, x), tensor: 4 (over y, core).
Axes of the slice: x: 2, y: 2, z: 4, core: 2. Of those that a mesh axis runs over, the one named last changes fastest.
Arguments:
- tokens: bfloat16 [16, 1024, 1536], P(None, 'dp', 'tensor'), may hold values from -6 to 6
- out_grad: bfloat16 [10240, 1536], P('dp', 'tensor'), may hold values from -6 to 6
- lengths: int32 [16], replicated, may hold values from 1 to 1024, as said below
- deal: int32 [16], replicated, may hold values from 0 to 15, as said below
- mixer_gain: bfloat16 [1536], P(('tensor', 'dp')), may hold values from 0.5 to 1.5
- inner_weight: bfloat16 [1536, 3072], P('dp', 'tensor'), may hold values from -0.15625 to 0.15625
- gate_weight: bfloat16 [1536, 3072], P('dp', 'tensor'), may hold values from -0.15625 to 0.15625
- conv_taps: bfloat16 [4, 3072], P(None, ('tensor', 'dp')), may hold values from -3 to 3
- conv_bias: bfloat16 [3072], P(('tensor', 'dp')), may hold values from -3 to 3
- proj_weight: bfloat16 [3072, 128], P(('tensor', 'dp')), may hold values from -0.109375 to 0.109375
- proj_gains: bfloat16 [128], P('dp'), may hold values from 0.5 to 1.5
- step_weight: bfloat16 [96, 128], P(None, ('tensor', 'dp')), may hold values from -0.625 to 0.625
- step_bias: bfloat16 [128], P(('tensor', 'dp')), may hold values from -6 to -2.5
- log_rate: bfloat16 [128], P(('tensor', 'dp')), may hold values from -0.5 to 1
- skip_gain: bfloat16 [3072], P(('tensor', 'dp')), may hold values from 0.5 to 1.5
- out_weight: bfloat16 [3072, 1536], P('tensor', 'dp'), may hold values from -0.3125 to 0.3125
- ffn_gain: bfloat16 [1536], P(('tensor', 'dp')), may hold values from 0.5 to 1.5
- ffn_gate: bfloat16 [1536, 4096], P('dp', 'tensor'), may hold values from -0.15625 to 0.15625
- ffn_up: bfloat16 [1536, 4096], P('dp', 'tensor'), may hold values from -0.15625 to 0.15625
- ffn_down: bfloat16 [4096, 1536], P('tensor', 'dp'), may hold values from -0.1875 to 0.1875
Outputs:
- output: bfloat16 [10240, 1536], P('dp', 'tensor')
- tokens_grad: bfloat16 [16, 1024, 1536], P(None, 'dp', 'tensor')
- grad_mixer_gain: float32 [1536], P(('tensor', 'dp'))
- grad_inner_weight: float32 [1536, 3072], P('dp', 'tensor')
- grad_gate_weight: float32 [1536, 3072], P('dp', 'tensor')
- grad_conv_taps: float32 [4, 3072], P(None, ('tensor', 'dp'))
- grad_conv_bias: float32 [3072], P(('tensor', 'dp'))
- grad_proj_weight: float32 [3072, 128], P(('tensor', 'dp'))
- grad_proj_gains: float32 [128], P('dp')
- grad_step_weight: float32 [96, 128], P(None, ('tensor', 'dp'))
- grad_step_bias: float32 [128], P(('tensor', 'dp'))
- grad_log_rate: float32 [128], P(('tensor', 'dp'))
- grad_skip_gain: float32 [3072], P(('tensor', 'dp'))
- grad_out_weight: float32 [3072, 1536], P('tensor', 'dp')
- grad_ffn_gain: float32 [1536], P(('tensor', 'dp'))
- grad_ffn_gate: float32 [1536, 4096], P('dp', 'tensor')
- grad_ffn_up: float32 [1536, 4096], P('dp', 'tensor')
- grad_ffn_down: float32 [4096, 1536], P('tensor', 'dp')
The draws below stay inside these ranges and needn't reach their ends.
Inputs may be any that keep to these rules, and one draw needn't show every extreme that they name: In deal order the sequences come in pairs whose lengths add up to at most 1280, the first of a pair being at least 512 long; so the 2 sequences dealt to one dp index fill at most 1280 packed rows, and in every draw the rows of one dp index are all filled and some sequence is exactly 1024 long. `deal`: A permutation of the sequence indices.
All inputs are finite; a program needn't handle non-finite values.
Results may differ from the reference program's by a relative error of at most 0.022.
Values may be sent and summed in bfloat16 or wider, within the bound.
No kernel may reach another device: no remote copies, remote signals or barrier semaphores. Data moves between devices by JAX's collectives and lax.ppermute only.
A program may use at most 256 MiB of HBM per device.

```python
import jax
import jax.numpy as jnp
from jax import lax

D = 1536
E = 3072
NS = 16
KC = 4
R = 96
F = 4096
HD = 24
HEADS = 128
LMAX = 1024
PAIRS = 1
SPG = 2
GCAP = 1280
SEQS = 16
ROWS = 10240


def deal_plan(key):
    base = jax.random.fold_in(key, 11)
    key_first, key_full, key_second, key_order = jax.random.split(base, 4)
    group_count = SEQS // SPG
    long_first = jax.random.randint(key_first, (group_count, PAIRS), LMAX // 2, LMAX + 1, dtype=jnp.int32)
    full_group = jax.random.randint(key_full, (), 0, group_count, dtype=jnp.int32)
    is_full = jnp.arange(group_count, dtype=jnp.int32)[:, None] == full_group
    first_pair = jnp.arange(PAIRS, dtype=jnp.int32)[None, :] == 0
    long_first = jnp.where(is_full & first_pair, LMAX, long_first)
    room_left = LMAX + LMAX // 4 - long_first
    fraction = jax.random.randint(key_second, (group_count, PAIRS), 0, 1 << 20, dtype=jnp.int32)
    second = 1 + fraction * room_left // (1 << 20)
    second = jnp.where(is_full, room_left, second)
    packed = jnp.stack([long_first, second], axis=2).reshape(SEQS).astype(jnp.int32)
    dealing = jax.random.permutation(key_order, SEQS).astype(jnp.int32)
    seq_lengths = jnp.zeros((SEQS,), jnp.int32).at[dealing].set(packed)
    return (seq_lengths, dealing)


def draw_lengths(key, part):
    return deal_plan(key)[0]


def draw_deal(key, part):
    return deal_plan(key)[1]


def block_scale(rng, shape, cuts, smallest, top_value):
    def one(dim, shards_of):
        steps = jax.random.uniform(jax.random.fold_in(jax.random.fold_in(rng, 6), dim), (shards_of,), jnp.float32, smallest / len(cuts), top_value / len(cuts))
        return jnp.repeat(jnp.exp(steps), shape[dim] // shards_of).reshape((-1,) + (1,) * (len(shape) - dim - 1))

    loudness = one(*cuts[0])
    for cut in cuts[1:]:
        loudness = loudness * one(*cut)
    return loudness


def scatter_about(own_key, shape, deviation, most, cuts=(), kind=jnp.bfloat16):
    values = jax.random.normal(own_key, shape, jnp.float32) * deviation
    if len(cuts) > 0:
        values = block_scale(own_key, shape, cuts, -0.22, 0.18) * values
    return jnp.clip(values, min=-most, max=most).astype(kind)


def setup_inputs(seed: int = 0) -> dict:
    splits = jax.random.split(jax.random.key(seed), 21)
    return {
        "tokens": scatter_about(splits[0], (SEQS, LMAX, D), 1.0, 6.0, ((1, 8), (2, 4))),
        "out_grad": scatter_about(splits[1], (ROWS, D), 1.0, 6.0, ((0, 8), (1, 4))),
        "lengths": draw_lengths(jax.random.fold_in(splits[20], 71), 0),
        "deal": draw_deal(jax.random.fold_in(splits[20], 71), 0),
        "mixer_gain": jnp.clip(1.0 + 0.1 * jax.random.normal(splits[4], (D,), jnp.float32), 0.5, 1.5).astype(jnp.bfloat16),
        "inner_weight": scatter_about(splits[5], (D, E), D ** -0.5, 0.15625, ((0, 8), (1, 4))),
        "gate_weight": scatter_about(splits[6], (D, E), D ** -0.5, 0.15625, ((0, 8), (1, 4))),
        "conv_taps": scatter_about(splits[7], (KC, E), KC ** -0.5, 3.0, ((1, 32),)),
        "conv_bias": scatter_about(splits[8], (E,), 0.5, 3.0, ((0, 32),)),
        "proj_weight": scatter_about(splits[9], (E, R + 2 * NS), E ** -0.5, 0.109375, ((0, 32),)),
        "proj_gains": jnp.clip(1.0 + 0.1 * jax.random.normal(splits[10], (R + 2 * NS,), jnp.float32), 0.5, 1.5).astype(jnp.bfloat16),
        "step_weight": scatter_about(splits[11], (R, HEADS), R ** -0.5, 0.625, ((1, 32),)),
        "step_bias": jnp.clip(-6.0 + 3.5 * jax.random.uniform(splits[12], (HEADS,), jnp.float32) ** block_scale(splits[12], (HEADS,), ((0, 32),), -0.2, 0.2), -6.0, -2.5).astype(jnp.bfloat16),
        "log_rate": jnp.clip(-0.5 + 1.5 * jax.random.uniform(splits[13], (HEADS,), jnp.float32) ** block_scale(splits[13], (HEADS,), ((0, 32),), -0.2, 0.2), -0.5, 1.0).astype(jnp.bfloat16),
        "skip_gain": jnp.clip(0.5 + 1.0 * jax.random.uniform(splits[14], (E,), jnp.float32) ** block_scale(splits[14], (E,), ((0, 32),), -0.2, 0.2), 0.5, 1.5).astype(jnp.bfloat16),
        "out_weight": scatter_about(splits[15], (E, D), (E // 8) ** -0.5, 0.3125, ((0, 4), (1, 8))),
        "ffn_gain": jnp.clip(1.0 + 0.1 * jax.random.normal(splits[16], (D,), jnp.float32), 0.5, 1.5).astype(jnp.bfloat16),
        "ffn_gate": scatter_about(splits[17], (D, F), D ** -0.5, 0.15625, ((0, 8), (1, 4))),
        "ffn_up": scatter_about(splits[18], (D, F), D ** -0.5, 0.15625, ((0, 8), (1, 4))),
        "ffn_down": scatter_about(splits[19], (F, D), (F // 4) ** -0.5, 0.1875, ((0, 4), (1, 8))),
    }


HIGHEST = lax.Precision.HIGHEST
EPSILON = 1e-06

@jax.custom_vjp
def low(v):
    return lax.optimization_barrier(v.astype(jnp.bfloat16)).astype(jnp.float32)

@jax.custom_vjp
def low_back(v):
    return v

def low_keep(v):
    return (low(v), None)

def low_pass(kept, grad):
    return (grad,)

def back_keep(v):
    return (v, None)

def back_low(kept, grad):
    return (low(grad),)
low.defvjp(low_keep, low_pass)
low_back.defvjp(back_keep, back_low)

def matmul_high(left, right):
    return jnp.dot(left, right, precision=HIGHEST)

def norm_rows(values, gain_part):
    return values * lax.rsqrt(lax.optimization_barrier(jnp.mean(values * values, axis=-1, keepdims=True)) + EPSILON) * gain_part

def sequence_forward(seq_in, params, live_rows):
    mixer_gain, inner_weight, gate_weight, conv_taps, conv_bias, proj_weight, proj_gains, step_weight, step_bias, log_rate, skip_gain, out_weight, ffn_gain, ffn_gate, ffn_up, ffn_down = params
    mixer_in = low(norm_rows(seq_in, mixer_gain))
    inner_pre = low_back(matmul_high(mixer_in, inner_weight))
    gate_pre = low_back(matmul_high(mixer_in, gate_weight))
    padded_inner = jnp.concatenate([jnp.zeros((KC - 1, inner_pre.shape[1]), jnp.float32), inner_pre], axis=0)
    conv_sum = conv_bias + jnp.zeros_like(inner_pre)
    for tap in range(KC):
        conv_sum = conv_sum + conv_taps[tap] * padded_inner[tap:tap + LMAX]
    conv_out = low(jax.nn.silu(conv_sum))
    projected = low_back(matmul_high(conv_out, proj_weight))
    step_low = norm_rows(projected[:, :R], proj_gains[:R])
    input_b = norm_rows(projected[:, R:R + NS], proj_gains[R:R + NS])
    output_c = norm_rows(projected[:, R + NS:], proj_gains[R + NS:])
    steps = jax.nn.softplus(matmul_high(step_low, step_weight) + step_bias)
    decays = jnp.exp(-steps * jnp.exp(log_rate))
    heads_in = conv_out.reshape(LMAX, HEADS, HD)

    def scan_step(ssm_state, pieces):
        step_decay, step_size, input_now, output_now, head_values = pieces
        ssm_state = step_decay[:, None, None] * ssm_state + step_size[:, None, None] * input_now[None, :, None] * head_values[:, None, :]
        return (ssm_state, jnp.einsum('n,hnp->hp', output_now, ssm_state, precision=HIGHEST))
    unused, scanned = lax.scan(scan_step, jnp.zeros((HEADS, NS, HD), jnp.float32), (decays, steps, input_b, output_c, heads_in))
    mixed_out = scanned.reshape(LMAX, E) + skip_gain * conv_out
    gated = low(mixed_out * jax.nn.silu(gate_pre))
    branch = low_back(matmul_high(gated, out_weight))
    residual = seq_in + branch
    ffn_in = low(norm_rows(residual, ffn_gain))
    gate_ffn = low_back(matmul_high(ffn_in, ffn_gate))
    up_ffn = low_back(matmul_high(ffn_in, ffn_up))
    hidden = low(jax.nn.silu(gate_ffn) * up_ffn)
    ffn_out = low_back(matmul_high(hidden, ffn_down))
    return (residual + ffn_out) * live_rows[:, None]

def reference(tokens, out_grad, lengths, deal, mixer_gain, inner_weight, gate_weight, conv_taps, conv_bias, proj_weight, proj_gains, step_weight, step_bias, log_rate, skip_gain, out_weight, ffn_gain, ffn_gate, ffn_up, ffn_down):
    params = tuple((weight.astype(jnp.float32) for weight in (mixer_gain, inner_weight, gate_weight, conv_taps, conv_bias, proj_weight, proj_gains, step_weight, step_bias, log_rate, skip_gain, out_weight, ffn_gain, ffn_gate, ffn_up, ffn_down)))
    seq_count = tokens.shape[0]
    seq_ids = jnp.arange(seq_count, dtype=jnp.int32)
    inverse = jnp.zeros((seq_count,), jnp.int32).at[deal].set(seq_ids)
    packed_lengths = lengths[deal].reshape(-1, SPG)
    group_starts = jnp.cumsum(packed_lengths, axis=1) - packed_lengths
    row_start = seq_ids // SPG * GCAP + group_starts.reshape(-1)
    padded_grad = jnp.concatenate([out_grad.astype(jnp.float32), jnp.zeros((LMAX, D), jnp.float32)], axis=0)
    position = jnp.arange(LMAX, dtype=jnp.int32)

    def one_sequence(totals, seq_index):
        live_rows = (position < lengths[seq_index]).astype(jnp.float32)
        cotangent = padded_grad[row_start[inverse[seq_index]] + position] * live_rows[:, None]
        seq_in = tokens[seq_index].astype(jnp.float32)
        result, pullback = jax.vjp(lambda first_in, param_in: sequence_forward(first_in, param_in, live_rows), seq_in, params)
        seq_grad, param_grads = pullback(cotangent)
        totals = jax.tree.map(lambda left, right: left + right, totals, param_grads)
        return (totals, (result, seq_grad))
    initial = tuple((jnp.zeros_like(weight) for weight in params))
    totals, (seq_outputs, seq_grads) = lax.scan(one_sequence, initial, seq_ids)
    row_ids = jnp.arange(ROWS, dtype=jnp.int32)
    group_of = row_ids // GCAP
    within = row_ids % GCAP
    row_starts = group_starts[group_of]
    filled = lax.optimization_barrier(jnp.sum(packed_lengths, axis=1))[group_of]
    live = within < filled
    slot = lax.optimization_barrier(jnp.sum((within[:, None] >= row_starts).astype(jnp.int32), axis=1)) - 1
    slot = jnp.where(live, slot, 0)
    offset = within - jnp.take_along_axis(row_starts, slot[:, None], axis=1)[:, 0]
    source = deal[group_of * SPG + slot]
    flat_rows = seq_outputs.reshape(-1, D)
    output = jnp.where(live[:, None], flat_rows[jnp.where(live, source * LMAX + offset, 0)], 0.0)
    return (output.astype(jnp.bfloat16), seq_grads.astype(jnp.bfloat16), totals[0], totals[1], totals[2], totals[3], totals[4], totals[5], totals[6], totals[7], totals[8], totals[9], totals[10], totals[11], totals[12], totals[13], totals[14], totals[15])
```

```python
import functools

import jax
import jax.numpy as jnp
from jax import lax
from jax.experimental import pallas as pl
from jax.experimental.pallas import tpu as pltpu
from jax.sharding import PartitionSpec as P

D = 1536
NS = 16
KC = 4
R = 96
LMAX = 1024
SPG = 2
GCAP = 1280
HEAD_WIDTH = 24


HIGHEST = lax.Precision.HIGHEST
EPSILON = 1e-06


def contract(left, right, left_dim, right_dim):
    return lax.dot_general(
        left, right, (((left_dim,), (right_dim,)), ((), ())), preferred_element_type=jnp.float32
    )


def conv_silu(inner_pre, conv_taps, conv_bias, segment):
    row_count = inner_pre.shape[0]
    running_sum = conv_bias + conv_taps[KC - 1] * inner_pre
    for offset in range(1, KC):
        earlier = jnp.concatenate(
            [
                jnp.zeros((offset, inner_pre.shape[1]), inner_pre.dtype),
                inner_pre[: row_count - offset],
            ],
            axis=0,
        )
        linked = jnp.concatenate(
            [jnp.zeros((offset,), jnp.bool_), segment[offset:] == segment[: row_count - offset]]
        )
        running_sum = running_sum + conv_taps[KC - 1 - offset] * jnp.where(
            linked[:, None], earlier, 0.0
        )
    return jax.nn.silu(running_sum)


LANES = 128
CHUNK = 128


def mixed_dot(left, right, left_dim=1, right_dim=0):
    return lax.dot_general(
        left.astype(jnp.bfloat16),
        right.astype(jnp.bfloat16),
        (((left_dim,), (right_dim,)), ((), ())),
        preferred_element_type=jnp.float32,
    )


def fine_dot(left, right, left_dim=1, right_dim=0):
    left_high, right_high = left.astype(jnp.bfloat16), right.astype(jnp.bfloat16)
    left_low = (left - left_high.astype(jnp.float32)).astype(jnp.bfloat16)
    right_low = (right - right_high.astype(jnp.float32)).astype(jnp.bfloat16)
    return (
        mixed_dot(left_high, right_high, left_dim, right_dim)
        + mixed_dot(left_high, right_low, left_dim, right_dim)
        + mixed_dot(left_low, right_high, left_dim, right_dim)
    )


def exact_dot(left, right, left_dim=1, right_dim=0):
    return lax.dot_general(
        left,
        right,
        (((left_dim,), (right_dim,)), ((), ())),
        precision=HIGHEST,
        preferred_element_type=jnp.float32,
    )


def split_dot(values, zero_one, right_dim, terms):
    total = None
    rest = values
    for term in range(terms):
        part = rest.astype(jnp.bfloat16)
        product = mixed_dot(part, zero_one, 1, right_dim)
        total = product if total is None else total + product
        if term + 1 < terms:
            rest = rest - part.astype(jnp.float32)
    return total


def tile_heads(tile, head_width, channel_count):
    first = tile * LANES
    heads = []
    for head in range(channel_count // head_width):
        low = max(head * head_width - first, 0)
        high = min((head + 1) * head_width - first, LANES)
        if low < high:
            heads.append((head, low, high))
    return heads


def chunk_setup(bounds_ref, chunk_index, proj, params_ref, step_w):
    first_row = chunk_index * CHUNK
    row_axis = lax.broadcasted_iota(jnp.int32, (CHUNK, LANES), 0)
    lane_axis = lax.broadcasted_iota(jnp.int32, (CHUNK, LANES), 1)

    def segment_of(position):
        result = jnp.int32(0)
        for edge in range(SPG):
            result = result + (position >= bounds_ref[edge]).astype(jnp.int32)
        return result

    row_seg = segment_of(row_axis + first_row)
    lane_seg = segment_of(lane_axis + first_row)
    seg_in = segment_of(jnp.maximum(first_row - 1, 0))
    seg_last = segment_of(first_row + CHUNK - 1)
    same = row_seg == lane_seg
    lower = row_axis >= lane_axis
    carried = (row_seg == seg_in).astype(jnp.float32)
    tail = (row_seg == seg_last).astype(jnp.float32)
    keep = (seg_last == seg_in).astype(jnp.float32)

    def group_of(index):
        return (index >= R).astype(jnp.int32) + (index >= R + NS).astype(jnp.int32)

    group_row, group_lane = group_of(row_axis), group_of(lane_axis)
    group_mean = jnp.where(
        group_row == group_lane, jnp.where(group_lane == 0, 1.0 / R, 1.0 / NS), 0.0
    )
    gains = params_ref[0:1, :]
    step_b = params_ref[1:2, :]
    rate = jnp.exp(params_ref[2:3, :])
    scale = lax.rsqrt(exact_dot(proj * proj, group_mean) + EPSILON)
    unit = proj * scale
    normed = unit * gains
    step_pre = exact_dot(normed, step_w) + step_b
    step_size = jnp.maximum(step_pre, 0.0) + jnp.log1p(jnp.exp(-jnp.abs(step_pre)))
    log_decay = -step_size * rate
    cumulative = exact_dot(lower.astype(jnp.float32), log_decay)
    low_lanes = lane_axis < NS
    input_b = jnp.where(low_lanes, pltpu.roll(normed, LANES - R, 1), 0.0)
    output_c = jnp.where(low_lanes, pltpu.roll(normed, LANES - R - NS, 1), 0.0)
    last = cumulative[CHUNK - 1 : CHUNK, :]
    return dict(
        lane_axis=lane_axis,
        same=same,
        lower=lower,
        group_mean=group_mean,
        gains=gains,
        rate=rate,
        scale=scale,
        unit=unit,
        normed=normed,
        step_pre=step_pre,
        step_size=step_size,
        log_decay=log_decay,
        cumulative=cumulative,
        input_b=input_b,
        output_c=output_c,
        head_in=jnp.exp(cumulative) * carried,
        head_out=jnp.exp(last - cumulative) * tail,
        head_keep=jnp.exp(last) * keep,
    )


def scan_forward_kernel(
    head_width,
    bounds_ref,
    proj_ref,
    conv_ref,
    gate_ref,
    params_ref,
    step_w_ref,
    skip_ref,
    expand_ref,
    gated_ref,
    scanned_ref,
    states_ref,
    state_ref,
):
    chunk_index = pl.program_id(0)

    @pl.when(chunk_index == 0)
    def _():
        state_ref[...] = jnp.zeros_like(state_ref)

    state = state_ref[...]
    states_ref[0] = state
    prep = chunk_setup(bounds_ref, chunk_index, proj_ref[...], params_ref, step_w_ref[...])
    expand = expand_ref[...]
    channel_count = conv_ref.shape[1]
    conv_in = conv_ref[...].astype(jnp.float32)
    weighted = split_dot(prep["step_size"], expand, 0, 2) * conv_in
    weighted_parts = [weighted.astype(jnp.bfloat16)]
    weighted_parts.append((weighted - weighted_parts[0].astype(jnp.float32)).astype(jnp.bfloat16))
    tail_values = split_dot(prep["head_out"], expand, 0, 2) * weighted
    keep = split_dot(jnp.broadcast_to(prep["head_keep"], (8, LANES)), expand, 0, 2)[0:1, :]
    b_rows = prep["input_b"].T[0:NS, :]
    state_ref[...] = keep * state + fine_dot(b_rows, tail_values)
    scores = exact_dot(prep["output_c"], prep["input_b"], 1, 1)
    scores = jnp.where(prep["same"] & prep["lower"], scores, 0.0)
    from_state = split_dot(prep["head_in"], expand, 0, 2) * fine_dot(
        prep["output_c"][:, 0:NS], state
    )
    cumulative = prep["cumulative"]
    cumulative_t = cumulative.T
    lane_axis = prep["lane_axis"]
    for tile in range(channel_count // LANES):
        columns = slice(tile * LANES, (tile + 1) * LANES)
        parts = [part[:, columns] for part in weighted_parts]
        mixing, masked = [], [[], []]
        for head, low, high in tile_heads(tile, head_width, channel_count):
            spread = cumulative[:, head : head + 1] - cumulative_t[head : head + 1, :]
            mixing.append((scores * jnp.exp(jnp.minimum(spread, 0.0))).astype(jnp.bfloat16))
            own = (lane_axis >= low) & (lane_axis < high)
            for part, kept in zip(parts, masked):
                kept.append(jnp.where(own, part, jnp.zeros_like(part)))
        mixing = jnp.concatenate(mixing, axis=1)
        inside = mixed_dot(mixing, jnp.concatenate(masked[0], axis=0)) + mixed_dot(
            mixing, jnp.concatenate(masked[1], axis=0)
        )
        scanned = inside + from_state[:, columns]
        scanned_ref[:, columns] = scanned
        gate = gate_ref[:, columns].astype(jnp.float32)
        mixed_out = scanned + skip_ref[:, columns] * conv_in[:, columns]
        gated_ref[:, columns] = (mixed_out * (gate / (1.0 + jnp.exp(-gate)))).astype(jnp.bfloat16)


def scan_backward_kernel(
    head_width,
    bounds_ref,
    upstream_ref,
    proj_ref,
    conv_ref,
    gate_ref,
    scanned_ref,
    states_ref,
    params_ref,
    step_w_ref,
    skip_ref,
    expand_ref,
    proj_grad_ref,
    conv_grad_ref,
    gate_grad_ref,
    step_w_grad_ref,
    rows_grad_ref,
    skip_grad_ref,
    state_grad_ref,
):
    step = pl.program_id(0)
    chunk_index = pl.num_programs(0) - 1 - step

    @pl.when(step == 0)
    def _():
        state_grad_ref[...] = jnp.zeros_like(state_grad_ref)
        step_w_grad_ref[...] = jnp.zeros_like(step_w_grad_ref)
        rows_grad_ref[...] = jnp.zeros_like(rows_grad_ref)
        skip_grad_ref[...] = jnp.zeros_like(skip_grad_ref)

    state = states_ref[0]
    state_grad = state_grad_ref[...]
    step_w = step_w_ref[...]
    prep = chunk_setup(bounds_ref, chunk_index, proj_ref[...], params_ref, step_w)
    expand = expand_ref[...]
    channel_count = conv_ref.shape[1]
    conv_in = conv_ref[...].astype(jnp.float32)
    step_wide = split_dot(prep["step_size"], expand, 0, 2)
    weighted = step_wide * conv_in
    weighted_low = weighted.astype(jnp.bfloat16)
    out_wide = split_dot(prep["head_out"], expand, 0, 2)
    in_wide = split_dot(prep["head_in"], expand, 0, 2)
    keep = split_dot(jnp.broadcast_to(prep["head_keep"], (8, LANES)), expand, 0, 2)[0:1, :]
    tail_values = out_wide * weighted
    b_rows = prep["input_b"].T[0:NS, :]
    c_rows = prep["output_c"].T[0:NS, :]
    state_out = keep * state + fine_dot(b_rows, tail_values)

    gate = gate_ref[...].astype(jnp.float32)
    upstream = upstream_ref[...].astype(jnp.float32)
    scanned = scanned_ref[...]
    logistic = 1.0 / (1.0 + jnp.exp(-gate))
    mixed_grad = upstream * (gate * logistic)
    mixed_out = scanned + skip_ref[...] * conv_in
    gate_grad_ref[...] = (
        upstream * mixed_out * (logistic * (1.0 + gate * (1.0 - logistic)))
    ).astype(jnp.bfloat16)
    skip_grad_ref[0:1, :] += jnp.sum(mixed_grad * conv_in, axis=0, keepdims=True)
    grad_low = mixed_grad.astype(jnp.bfloat16)
    grad_round = grad_low.astype(jnp.float32)

    pad_rows = jnp.zeros((LANES - NS, channel_count), jnp.float32)
    state_tall = jnp.concatenate([state, pad_rows], axis=0)
    state_grad_tall = jnp.concatenate([state_grad, pad_rows], axis=0)
    from_in = in_wide * grad_round
    c_grad = mixed_dot(from_in, state_tall, 1, 1)
    b_grad = mixed_dot(tail_values, state_grad_tall, 1, 1)
    weighted_grad = out_wide * fine_dot(prep["input_b"][:, 0:NS], state_grad)
    state_grad_ref[...] = keep * state_grad + fine_dot(c_rows, from_in)

    row_axis = lax.broadcasted_iota(jnp.int32, (CHUNK, LANES), 0)
    upper = prep["same"] & (row_axis <= prep["lane_axis"])
    scores_t = jnp.where(upper, exact_dot(prep["input_b"], prep["output_c"], 1, 1), 0.0)
    cumulative = prep["cumulative"]
    cumulative_t = cumulative.T
    lane_axis = prep["lane_axis"]
    scores_grad = jnp.zeros((CHUNK, LANES), jnp.float32)
    inside_grads = []
    for tile in range(channel_count // LANES):
        columns = slice(tile * LANES, (tile + 1) * LANES)
        values = weighted_low[:, columns]
        grads = grad_low[:, columns]
        mixing, masked_values, masked_grads, decays = [], [], [], []
        for head, low, high in tile_heads(tile, head_width, channel_count):
            spread = cumulative_t[head : head + 1, :] - cumulative[:, head : head + 1]
            decay = jnp.exp(jnp.minimum(spread, 0.0))
            decays.append(decay)
            mixing.append((scores_t * decay).astype(jnp.bfloat16))
            own = (lane_axis >= low) & (lane_axis < high)
            masked_values.append(jnp.where(own, values, jnp.zeros_like(values)))
            masked_grads.append(jnp.where(own, grads, jnp.zeros_like(grads)))
        pair_grads = mixed_dot(jnp.concatenate(masked_values, axis=0), grads, 1, 1)
        for place, decay in enumerate(decays):
            scores_grad = scores_grad + decay * pair_grads[place * CHUNK : (place + 1) * CHUNK, :]
        inside_grads.append(
            mixed_dot(jnp.concatenate(mixing, axis=1), jnp.concatenate(masked_grads, axis=0))
        )
    weighted_grad = weighted_grad + jnp.concatenate(inside_grads, axis=1)
    scores_grad = jnp.where(upper, scores_grad, 0.0)
    b_grad = b_grad + mixed_dot(scores_grad, prep["output_c"])
    c_grad = c_grad + mixed_dot(scores_grad.T, prep["input_b"])
    conv_grad_ref[...] = mixed_grad * skip_ref[...] + weighted_grad * step_wide
    spread_grad = split_dot(
        grad_round * scanned - weighted * weighted_grad, expand, 1, 3
    )
    edge = jnp.broadcast_to(
        jnp.sum(state_out * state_grad, axis=0, keepdims=True), (8, channel_count)
    )
    edge_grad = split_dot(edge, expand, 1, 3)[0:1, :]
    spread_grad = spread_grad + jnp.where(row_axis == CHUNK - 1, edge_grad, 0.0)
    decay_grad = exact_dot((row_axis <= lane_axis).astype(jnp.float32), spread_grad)
    step_grad = split_dot(weighted_grad * conv_in, expand, 1, 2) - decay_grad * prep["rate"]
    step_pre = prep["step_pre"]
    pre_grad = step_grad / (1.0 + jnp.exp(-step_pre))
    step_w_grad_ref[...] += exact_dot(prep["normed"].T, pre_grad)
    normed_grad = (
        exact_dot(pre_grad, step_w, 1, 1)
        + pltpu.roll(b_grad, R, 1)
        + pltpu.roll(c_grad, R + NS, 1)
    )
    unit = prep["unit"]
    rows_grad_ref[0:1, :] += jnp.sum(normed_grad * unit, axis=0, keepdims=True)
    rows_grad_ref[1:2, :] += jnp.sum(pre_grad, axis=0, keepdims=True)
    rows_grad_ref[2:3, :] += jnp.sum(decay_grad * prep["log_decay"], axis=0, keepdims=True)
    unit_grad = normed_grad * prep["gains"]
    along = exact_dot(unit_grad * unit, prep["group_mean"], 1, 1)
    proj_grad_ref[...] = prep["scale"] * (unit_grad - unit * along)


def scan_operands(step_weight, step_bias, log_rate, skip_gain, proj_gains, head_width):
    head_count = step_bias.shape[0]
    channel_count = skip_gain.shape[0]

    def lane_row(values):
        return jnp.pad(values.astype(jnp.float32), (0, LANES - values.shape[0]))[None, :]

    params = jnp.concatenate(
        [
            lane_row(proj_gains),
            lane_row(step_bias),
            lane_row(log_rate),
            jnp.zeros((5, LANES), jnp.float32),
        ],
        axis=0,
    )
    step_w = jnp.pad(
        step_weight.astype(jnp.float32), ((0, LANES - R), (0, LANES - head_count))
    )
    skip = skip_gain.astype(jnp.float32)[None, :]
    owner = lax.broadcasted_iota(jnp.int32, (LANES, channel_count), 1) // head_width
    head = lax.broadcasted_iota(jnp.int32, (LANES, channel_count), 0)
    return params, step_w, skip, (owner == head).astype(jnp.bfloat16)


def whole(shape):
    return pl.BlockSpec(shape, lambda i, *_: (0,) * len(shape))


def scan_forward(bounds, projected, conv_out, gate_pre, operands, head_width):
    params, step_w, skip, expand = operands
    rows, channels = conv_out.shape
    chunks = rows // CHUNK

    def chunk_rows(width):
        return pl.BlockSpec((CHUNK, width), lambda i, *_: (i, 0))

    return pl.pallas_call(
        functools.partial(scan_forward_kernel, head_width),
        out_shape=(
            jax.ShapeDtypeStruct((rows, channels), jnp.bfloat16),
            jax.ShapeDtypeStruct((rows, channels), jnp.float32),
            jax.ShapeDtypeStruct((chunks, NS, channels), jnp.float32),
        ),
        grid_spec=pltpu.PrefetchScalarGridSpec(
            num_scalar_prefetch=1,
            grid=(chunks,),
            in_specs=[
                chunk_rows(LANES),
                chunk_rows(channels),
                chunk_rows(channels),
                whole(params.shape),
                whole(step_w.shape),
                whole(skip.shape),
                whole(expand.shape),
            ],
            out_specs=[
                chunk_rows(channels),
                chunk_rows(channels),
                pl.BlockSpec((1, NS, channels), lambda i, *_: (i, 0, 0)),
            ],
            scratch_shapes=[pltpu.VMEM((NS, channels), jnp.float32)],
        ),
        cost_estimate=pl.CostEstimate(
            flops=40_000_000_000, bytes_accessed=14_000_000, transcendentals=6_000_000
        ),
        name="scan_forward",
    )(bounds, projected, conv_out, gate_pre, params, step_w, skip, expand)


def scan_backward(bounds, upstream, projected, conv_out, gate_pre, scanned, states, operands, head_width):
    params, step_w, skip, expand = operands
    rows, channels = conv_out.shape
    chunks = rows // CHUNK

    def chunk_rows(width):
        return pl.BlockSpec((CHUNK, width), lambda i, *_: (chunks - 1 - i, 0))

    return pl.pallas_call(
        functools.partial(scan_backward_kernel, head_width),
        out_shape=(
            jax.ShapeDtypeStruct((rows, LANES), jnp.float32),
            jax.ShapeDtypeStruct((rows, channels), jnp.float32),
            jax.ShapeDtypeStruct((rows, channels), jnp.bfloat16),
            jax.ShapeDtypeStruct((LANES, LANES), jnp.float32),
            jax.ShapeDtypeStruct((8, LANES), jnp.float32),
            jax.ShapeDtypeStruct((8, channels), jnp.float32),
        ),
        grid_spec=pltpu.PrefetchScalarGridSpec(
            num_scalar_prefetch=1,
            grid=(chunks,),
            in_specs=[
                chunk_rows(channels),
                chunk_rows(LANES),
                chunk_rows(channels),
                chunk_rows(channels),
                chunk_rows(channels),
                pl.BlockSpec((1, NS, channels), lambda i, *_: (chunks - 1 - i, 0, 0)),
                whole(params.shape),
                whole(step_w.shape),
                whole(skip.shape),
                whole(expand.shape),
            ],
            out_specs=[
                chunk_rows(LANES),
                chunk_rows(channels),
                chunk_rows(channels),
                whole((LANES, LANES)),
                whole((8, LANES)),
                whole((8, channels)),
            ],
            scratch_shapes=[pltpu.VMEM((NS, channels), jnp.float32)],
        ),
        cost_estimate=pl.CostEstimate(
            flops=80_000_000_000, bytes_accessed=24_000_000, transcendentals=8_000_000
        ),
        name="scan_backward",
    )(bounds, upstream, projected, conv_out, gate_pre, scanned, states, params, step_w, skip, expand)


PLACES = (0, 2, 1, 3)


def swap_pairs(size, flip):
    return [(index, index ^ flip) for index in range(size)]


class Wires:
    def __init__(self, dp_size, tensor_size):
        self.dp_size = dp_size
        self.tensor_size = tensor_size
        self.staged = tensor_size == 4 and dp_size == 8
        self.group = lax.axis_index("dp")
        self.lane = lax.axis_index("tensor")
        self.outer = self.group // 2
        self.inner = self.group % 2
        self.turn = jnp.bitwise_xor(self.lane, self.outer)

    def over_tensor(self, values, flip):
        return lax.ppermute(values, "tensor", swap_pairs(self.tensor_size, flip))

    def over_dp(self, values, flip):
        return lax.ppermute(values, "dp", swap_pairs(self.dp_size, flip))

    def place_of(self, distance):
        block = jnp.bitwise_xor(self.turn, distance)
        return (block & 1) * 2 + (block >> 1)


    def gather_features(self, values):
        if not self.staged:
            return lax.all_gather(values, "tensor", axis=1, tiled=True)
        across = self.over_tensor(values, 2)
        beside = self.over_tensor(values, 1)
        diagonal = self.over_tensor(across, 1)
        return jnp.concatenate([values, across, beside, diagonal], axis=1)

    def sum_features(self, project):
        width = D // self.tensor_size
        if not self.staged:
            return lax.psum_scatter(
                project(slice(0, D)), "tensor", scatter_dimension=1, tiled=True
            )
        sent = project(slice(2 * width, 4 * width)).astype(jnp.bfloat16)
        kept = project(slice(0, 2 * width))
        total = kept + self.over_tensor(sent, 1).astype(jnp.float32)
        across = self.over_tensor(total[:, width:].astype(jnp.bfloat16), 2)
        return total[:, :width] + across.astype(jnp.float32)

    def sum_small(self, values):
        if not self.staged:
            return lax.psum(values, "tensor")
        values = values + self.over_tensor(values, 1)
        return values + self.over_tensor(values, 2)

    def sum_rows(self, values, wire):
        if not self.staged:
            return lax.psum(values.astype(wire), "tensor").astype(jnp.float32)
        half = values.shape[0] // 2
        core = self.lane % 2
        kept = lax.dynamic_slice_in_dim(values, core * half, half)
        sent = lax.dynamic_slice_in_dim(values, (1 - core) * half, half)
        total = kept + self.over_tensor(sent.astype(wire), 1).astype(jnp.float32)
        total = total + self.over_tensor(total.astype(wire), 2).astype(jnp.float32)
        other = self.over_tensor(total.astype(wire), 1).astype(jnp.float32)
        total = total.astype(wire).astype(jnp.float32)
        first = jnp.where(core == 0, total, other)
        second = jnp.where(core == 0, other, total)
        return jnp.concatenate([first, second], axis=0)


    def gather_pieces(self, shard):
        same = [shard] + [self.over_dp(shard, 2 * distance) for distance in range(1, self.dp_size // 2)]
        return same, [self.over_dp(piece, 1) for piece in same]

    def gather_weights(self, shards):
        if not self.staged:
            return [lax.all_gather(shard, "dp", axis=0, tiled=True) for shard in shards], shards[0]
        widths = [shard.shape[1] for shard in shards]
        shard = shards[0] if len(shards) == 1 else jnp.concatenate(shards, axis=1)
        same, other = self.gather_pieces(shard)
        places = jnp.stack([self.place_of(distance) for distance in range(4)] + [self.inner])
        return arrange_weights(places.astype(jnp.int32), same, other, widths), other[3]

    def sum_weights(self, grad):
        if not self.staged:
            return lax.psum_scatter(
                grad.astype(jnp.bfloat16), "dp", scatter_dimension=0, tiled=True
            ).astype(jnp.float32)
        width = grad.shape[1]
        blocks = grad.reshape(4, 2, D // 8, width)
        sent = lax.dynamic_index_in_dim(blocks, 1 - self.inner, 1, keepdims=False)
        kept = lax.dynamic_index_in_dim(blocks, self.inner, 1, keepdims=False)
        got = self.over_dp(sent.astype(jnp.bfloat16), 1)
        total = (kept.astype(jnp.float32) + got.astype(jnp.float32)).astype(jnp.bfloat16)
        pieces = [
            lax.dynamic_index_in_dim(total, self.place_of(distance), 0, keepdims=False)
            for distance in range(4)
        ]
        result = pieces[0].astype(jnp.float32)
        for distance in range(1, 4):
            result = result + self.over_dp(pieces[distance], 2 * distance).astype(jnp.float32)
        return result

    def gather_rows(self, block):
        if not self.staged:
            return lax.all_gather(block, "dp", axis=0, tiled=False)
        same = jnp.stack(
            [block] + [self.over_dp(block, 2 * distance) for distance in range(1, 4)]
        )
        other = self.over_dp(same, 1)
        both = jnp.stack([same, other], axis=1).reshape((8,) + block.shape)
        index = jnp.arange(8, dtype=jnp.int32)
        return both[jnp.bitwise_xor(index, self.group)]

    def sum_blocks(self, blocks):
        if not self.staged:
            return lax.psum_scatter(blocks, "dp", scatter_dimension=0, tiled=False)
        paired = blocks.reshape((4, 2) + blocks.shape[1:])
        sent = lax.dynamic_index_in_dim(paired, 1 - self.inner, 1, keepdims=False)
        kept = lax.dynamic_index_in_dim(paired, self.inner, 1, keepdims=False)
        total = kept + self.over_dp(sent, 1)
        result = lax.dynamic_index_in_dim(total, self.outer, 0, keepdims=False)
        for distance in range(1, 4):
            piece = lax.dynamic_index_in_dim(
                total, jnp.bitwise_xor(self.outer, distance), 0, keepdims=False
            )
            result = result + self.over_dp(piece, 2 * distance)
        return result

    def exchange(self, blocks):
        got = [blocks[0]]
        for flip in range(1, self.dp_size):
            got.append(self.over_dp(blocks[flip], flip))
        return jnp.stack(got)


def arrange_kernel(widths, places_ref, *refs):
    same, other, outs = refs[:4], refs[4:8], refs[8:]
    step = pl.program_id(0)
    rows = same[0].shape[0]
    first = pl.multiple_of(places_ref[4] * rows, 16)
    second = pl.multiple_of((1 - places_ref[4]) * rows, 16)
    for distance in range(4):

        @pl.when(step == distance)
        def _(distance=distance):
            start = 0
            for out, width in zip(outs, widths):
                columns = slice(start, start + width)
                out[pl.ds(first, rows), :] = same[distance][:, columns]
                out[pl.ds(second, rows), :] = other[distance][:, columns]
                start += width


def arrange_weights(places, same, other, widths):
    rows, width = same[0].shape
    return pl.pallas_call(
        functools.partial(arrange_kernel, widths),
        out_shape=[jax.ShapeDtypeStruct((8 * rows, part), jnp.bfloat16) for part in widths],
        grid_spec=pltpu.PrefetchScalarGridSpec(
            num_scalar_prefetch=1,
            grid=(4,),
            in_specs=[whole((rows, width))] * 8,
            out_specs=[
                pl.BlockSpec((2 * rows, part), lambda i, places_ref: (places_ref[i], 0))
                for part in widths
            ],
        ),
        cost_estimate=pl.CostEstimate(
            flops=0, bytes_accessed=32 * rows * width, transcendentals=0
        ),
        name="arrange_weights",
    )(places, *same, *other)


def pack_rows(parts):
    blocks = parts[0].shape[0]
    flat = jnp.concatenate([part.reshape(blocks, -1) for part in parts], axis=1)
    size = flat.shape[1]
    rows = -(-size // (16 * LANES)) * 16
    flat = jnp.pad(flat, ((0, 0), (0, rows * LANES - size)))
    return flat.reshape(blocks, rows, LANES)


def unpack_rows(packed, shapes):
    blocks = packed.shape[0]
    flat = packed.reshape(blocks, -1)
    parts, start = [], 0
    for shape in shapes:
        size = 1
        for extent in shape:
            size *= extent
        parts.append(flat[:, start : start + size].reshape((blocks,) + shape))
        start += size
    return parts


def after(values, earlier):
    return lax.optimization_barrier((values, earlier))[0]


def row_scale(wires, values):
    mean_square = wires.sum_small(jnp.sum(values * values, axis=1).reshape(-1, LANES)) / D
    return lax.rsqrt(mean_square + EPSILON).reshape(-1)


def norm_back(wires, values, inverse, gain, upstream):
    normed = values * inverse[:, None]
    gain_grad = jnp.sum(upstream * normed, axis=0)
    scaled = upstream * gain
    along = jnp.sum(scaled * normed, axis=1).reshape(-1, LANES)
    along = wires.sum_small(along).reshape(-1) / D
    return inverse[:, None] * (scaled - normed * along[:, None]), gain_grad


def per_device(
    dp_size,
    tensor_size,
    tokens,
    out_grad,
    lengths,
    deal,
    mixer_gain,
    inner_weight,
    gate_weight,
    conv_taps,
    conv_bias,
    proj_weight,
    proj_gains,
    step_weight,
    step_bias,
    log_rate,
    skip_gain,
    out_weight,
    ffn_gain,
    ffn_gate,
    ffn_up,
    ffn_down,
):
    wires = Wires(dp_size, tensor_size)
    group = wires.group
    bf16, f32 = jnp.bfloat16, jnp.float32

    packed_lengths = lengths[deal]
    group_lengths = lax.dynamic_slice_in_dim(packed_lengths, group * SPG, SPG)
    starts = jnp.cumsum(group_lengths) - group_lengths
    filled = jnp.sum(group_lengths)
    bounds = jnp.concatenate([starts[1:], filled[None]]).astype(jnp.int32)
    row_ids = jnp.arange(GCAP, dtype=jnp.int32)
    live_rows = row_ids < filled
    segment = jnp.sum((row_ids[:, None] >= bounds[None, :]).astype(jnp.int32), axis=1)
    slot = jnp.minimum(segment, SPG - 1)
    position = row_ids - jnp.where(slot == 0, 0, starts[slot])
    span = LMAX // dp_size
    ranks = jnp.arange(dp_size, dtype=jnp.int32)
    source_rows = (
        jnp.bitwise_xor(position // span, group) * (SPG * span) + slot * span + position % span
    )
    source_rows = jnp.where(live_rows, source_rows, 0)

    dealt = deal.reshape(dp_size, SPG)[jnp.bitwise_xor(ranks, group)]
    arrived = wires.exchange(tokens[dealt.reshape(-1)].reshape((dp_size, SPG) + tokens.shape[1:]))
    flat_rows = arrived.reshape(dp_size * SPG * span, -1)
    packed = jnp.where(live_rows[:, None], flat_rows[source_rows], 0.0).astype(f32)

    small_shapes = [
        proj_weight.shape,
        mixer_gain.shape,
        conv_taps.shape,
        conv_bias.shape,
        proj_gains.shape,
        step_weight.shape,
        step_bias.shape,
        log_rate.shape,
        skip_gain.shape,
        ffn_gain.shape,
    ]
    small = pack_rows(
        [
            part[None]
            for part in (
                proj_weight,
                mixer_gain,
                conv_taps,
                conv_bias,
                proj_gains,
                step_weight,
                step_bias,
                log_rate,
                skip_gain,
                ffn_gain,
            )
        ]
    )[0]
    small = unpack_rows(wires.gather_rows(small), small_shapes)

    def along_last(part):
        return jnp.moveaxis(part, 0, -2).reshape(part.shape[1:-1] + (-1,))

    proj_all = small[0].reshape(-1, small[0].shape[-1])
    gain_all, taps_all, bias_all, gains_all, step_w_all, step_b_all, rate_all, skip_all, ffn_gain_all = [
        along_last(part).astype(f32) for part in small[1:]
    ]

    (inner_all, gate_all), mark = wires.gather_weights(
        list(after((inner_weight, gate_weight), arrived))
    )
    (out_all,), mark = wires.gather_weights([after(out_weight.T, mark)])
    (ffn_gate_all, ffn_up_all), mark = wires.gather_weights(
        list(after((ffn_gate, ffn_up), mark))
    )
    (ffn_down_all,), mark = wires.gather_weights([after(ffn_down.T, mark)])

    inverse_in = row_scale(wires, packed)
    mixer_rows = wires.gather_features((packed * inverse_in[:, None] * gain_all).astype(bf16))
    inner_pre = contract(mixer_rows, inner_all, 1, 0)
    gate_pre = contract(mixer_rows, gate_all, 1, 0)
    conv_out = conv_silu(inner_pre, taps_all, bias_all, segment).astype(bf16)
    projected = wires.sum_rows(contract(conv_out, proj_all, 1, 0), f32)
    operands = scan_operands(step_w_all, step_b_all, rate_all, skip_all, gains_all, HEAD_WIDTH)
    gated, scanned, states = scan_forward(
        bounds, projected, conv_out, gate_pre, operands, HEAD_WIDTH
    )
    residual = packed + wires.sum_features(lambda rows: contract(gated, out_all[rows], 1, 1))

    inverse_mid = row_scale(wires, residual)
    ffn_rows = wires.gather_features((residual * inverse_mid[:, None] * ffn_gain_all).astype(bf16))
    gate_ffn = contract(ffn_rows, ffn_gate_all, 1, 0)
    up_ffn = contract(ffn_rows, ffn_up_all, 1, 0)
    logistic = jax.nn.sigmoid(gate_ffn)
    activated = gate_ffn * logistic
    hidden = (activated * up_ffn).astype(bf16)
    final_rows = residual + wires.sum_features(
        lambda rows: contract(hidden, ffn_down_all[rows], 1, 1)
    )
    output = jnp.where(live_rows[:, None], final_rows, 0.0).astype(bf16)

    out_cot = jnp.where(live_rows[:, None], out_grad, 0.0).astype(bf16)
    cot_rows = wires.gather_features(out_cot)
    hidden_grad = contract(cot_rows, ffn_down_all, 1, 0)
    gate_grad = (hidden_grad * up_ffn * logistic * (1.0 + gate_ffn * (1.0 - logistic))).astype(bf16)
    up_grad = (hidden_grad * activated).astype(bf16)
    mid_grad = wires.sum_features(
        lambda rows: contract(gate_grad, ffn_gate_all[rows], 1, 1)
        + contract(up_grad, ffn_up_all[rows], 1, 1)
    )
    ffn_down_grad = wires.sum_weights(contract(cot_rows, hidden, 0, 0).astype(bf16)).T
    ffn_gate_grad = wires.sum_weights(contract(ffn_rows, gate_grad, 0, 0).astype(bf16))
    ffn_up_grad = wires.sum_weights(contract(ffn_rows, up_grad, 0, 0).astype(bf16))
    mid_back, ffn_gain_grad = norm_back(wires, residual, inverse_mid, ffn_gain_all, mid_grad)
    residual_grad = out_cot.astype(f32) + mid_back

    branch_rows = wires.gather_features(residual_grad.astype(bf16))
    gated_grad = contract(branch_rows, out_all, 1, 0)
    out_weight_grad = wires.sum_weights(contract(branch_rows, gated, 0, 0).astype(bf16)).T
    proj_part, conv_core_grad, gate_low, step_w_part, row_parts, skip_part = scan_backward(
        bounds, gated_grad, projected, conv_out, gate_pre, scanned, states, operands, HEAD_WIDTH
    )
    head_count = step_b_all.shape[0]
    gains_grad = wires.sum_small(row_parts)[0]
    proj_low = wires.sum_rows(proj_part, bf16).astype(bf16)
    conv_grad = conv_core_grad + contract(proj_low, proj_all, 1, 1)
    proj_weight_grad = contract(conv_out, proj_low, 0, 0)

    def conv_piece(inner_in, taps_in, bias_in):
        return conv_silu(inner_in, taps_in, bias_in, segment)

    unused_conv, conv_pull = jax.vjp(conv_piece, inner_pre, taps_all, bias_all)
    inner_grad, taps_grad, bias_grad = conv_pull(conv_grad)
    inner_low = inner_grad.astype(bf16)
    in_grad = wires.sum_features(
        lambda rows: contract(inner_low, inner_all[rows], 1, 1)
        + contract(gate_low, gate_all[rows], 1, 1)
    )
    gate_weight_grad = wires.sum_weights(contract(mixer_rows, gate_low, 0, 0).astype(bf16))
    inner_weight_grad = wires.sum_weights(contract(mixer_rows, inner_low, 0, 0).astype(bf16))
    in_back, mixer_gain_grad = norm_back(wires, packed, inverse_in, gain_all, in_grad)

    grad_packed = (residual_grad + in_back).astype(bf16)
    place = jnp.arange(span, dtype=jnp.int32)
    slot_position = (jnp.bitwise_xor(ranks, group) * span)[:, None, None] + place[None, None, :]
    slot_live = slot_position < group_lengths[None, :, None]
    slot_rows = jnp.where(slot_live, starts[None, :, None] + slot_position, 0).reshape(-1)
    leaving = jnp.where(slot_live.reshape(-1)[:, None], grad_packed[slot_rows], 0.0)
    returned = wires.exchange(leaving.reshape(dp_size, SPG, span, -1))
    inverse_deal = jnp.zeros_like(deal).at[deal].set(
        jnp.arange(deal.shape[0], dtype=jnp.int32)
    )
    came_from = jnp.bitwise_xor(inverse_deal // SPG, group) * SPG + inverse_deal % SPG
    tokens_grad = returned.reshape((dp_size * SPG, span, -1))[came_from]

    def by_index(part):
        split = part.reshape(part.shape[:-1] + (dp_size, part.shape[-1] // dp_size))
        return jnp.moveaxis(split, -2, 0)

    small_grads = pack_rows(
        [
            proj_weight_grad.reshape(dp_size, -1, proj_weight_grad.shape[1]),
            by_index(mixer_gain_grad),
            by_index(taps_grad),
            by_index(bias_grad),
            by_index(gains_grad),
            by_index(step_w_part[:R, :head_count]),
            by_index(row_parts[1, :head_count]),
            by_index(row_parts[2, :head_count]),
            by_index(skip_part[0]),
            by_index(ffn_gain_grad),
        ]
    )
    (
        proj_weight_grad,
        mixer_gain_grad,
        taps_grad,
        bias_grad,
        gains_grad,
        step_w_grad,
        step_b_grad,
        rate_grad,
        skip_grad,
        ffn_gain_grad,
    ) = [part[0] for part in unpack_rows(wires.sum_blocks(small_grads)[None], small_shapes)]
    return (
        output,
        tokens_grad,
        mixer_gain_grad,
        inner_weight_grad,
        gate_weight_grad,
        taps_grad,
        bias_grad,
        proj_weight_grad,
        gains_grad,
        step_w_grad,
        step_b_grad,
        rate_grad,
        skip_grad,
        out_weight_grad,
        ffn_gain_grad,
        ffn_gate_grad,
        ffn_up_grad,
        ffn_down_grad,
    )


def solution(mesh):
    return jax.shard_map(
        functools.partial(per_device, mesh.shape["dp"], mesh.shape["tensor"]),
        mesh=mesh,
        in_specs=(
            P(None, "dp", "tensor"),
            P("dp", "tensor"),
            P(),
            P(),
            P(("tensor", "dp")),
            P("dp", "tensor"),
            P("dp", "tensor"),
            P(None, ("tensor", "dp")),
            P(("tensor", "dp")),
            P(("tensor", "dp"), None),
            P("dp"),
            P(None, ("tensor", "dp")),
            P(("tensor", "dp")),
            P(("tensor", "dp")),
            P(("tensor", "dp")),
            P("tensor", "dp"),
            P(("tensor", "dp")),
            P("dp", "tensor"),
            P("dp", "tensor"),
            P("tensor", "dp"),
        ),
        out_specs=(
            P("dp", "tensor"),
            P(None, "dp", "tensor"),
            P(("tensor", "dp")),
            P("dp", "tensor"),
            P("dp", "tensor"),
            P(None, ("tensor", "dp")),
            P(("tensor", "dp")),
            P(("tensor", "dp"), None),
            P("dp"),
            P(None, ("tensor", "dp")),
            P(("tensor", "dp")),
            P(("tensor", "dp")),
            P(("tensor", "dp")),
            P("tensor", "dp"),
            P(("tensor", "dp")),
            P("dp", "tensor"),
            P("dp", "tensor"),
            P("tensor", "dp"),
        ),
        check_vma=False,
    )
```

```python
import functools

import jax
import jax.numpy as jnp
from jax import lax
from jax.experimental import pallas as pl
from jax.experimental.pallas import tpu as pltpu
from jax.sharding import PartitionSpec as P

D = 1536
NS = 16
KC = 4
R = 96
LMAX = 1024
SPG = 2
GCAP = 1280
HEAD_WIDTH = 24


HIGHEST = lax.Precision.HIGHEST
EPSILON = 1e-06


def contract(left, right, left_dim, right_dim):
    return lax.dot_general(
        left, right, (((left_dim,), (right_dim,)), ((), ())), preferred_element_type=jnp.float32
    )


def conv_silu(inner_pre, conv_taps, conv_bias, segment):
    row_count = inner_pre.shape[0]
    running_sum = conv_bias + conv_taps[KC - 1] * inner_pre
    for offset in range(1, KC):
        earlier = jnp.concatenate(
            [
                jnp.zeros((offset, inner_pre.shape[1]), inner_pre.dtype),
                inner_pre[: row_count - offset],
            ],
            axis=0,
        )
        linked = jnp.concatenate(
            [jnp.zeros((offset,), jnp.bool_), segment[offset:] == segment[: row_count - offset]]
        )
        running_sum = running_sum + conv_taps[KC - 1 - offset] * jnp.where(
            linked[:, None], earlier, 0.0
        )
    return jax.nn.silu(running_sum)


LANES = 128
CHUNK = 128


def mixed_dot(left, right, left_dim=1, right_dim=0):
    return lax.dot_general(
        left.astype(jnp.bfloat16),
        right.astype(jnp.bfloat16),
        (((left_dim,), (right_dim,)), ((), ())),
        preferred_element_type=jnp.float32,
    )


def fine_dot(left, right, left_dim=1, right_dim=0):
    left_high, right_high = left.astype(jnp.bfloat16), right.astype(jnp.bfloat16)
    left_low = (left - left_high.astype(jnp.float32)).astype(jnp.bfloat16)
    right_low = (right - right_high.astype(jnp.float32)).astype(jnp.bfloat16)
    return (
        mixed_dot(left_high, right_high, left_dim, right_dim)
        + mixed_dot(left_high, right_low, left_dim, right_dim)
        + mixed_dot(left_low, right_high, left_dim, right_dim)
    )


def exact_dot(left, right, left_dim=1, right_dim=0):
    return lax.dot_general(
        left,
        right,
        (((left_dim,), (right_dim,)), ((), ())),
        precision=HIGHEST,
        preferred_element_type=jnp.float32,
    )


def split_dot(values, zero_one, right_dim, terms):
    total = None
    rest = values
    for term in range(terms):
        part = rest.astype(jnp.bfloat16)
        product = mixed_dot(part, zero_one, 1, right_dim)
        total = product if total is None else total + product
        if term + 1 < terms:
            rest = rest - part.astype(jnp.float32)
    return total


def tile_heads(tile, head_width, channel_count):
    first = tile * LANES
    heads = []
    for head in range(channel_count // head_width):
        low = max(head * head_width - first, 0)
        high = min((head + 1) * head_width - first, LANES)
        if low < high:
            heads.append((head, low, high))
    return heads


def chunk_setup(bounds_ref, chunk_index, proj, params_ref, step_w):
    first_row = chunk_index * CHUNK
    row_axis = lax.broadcasted_iota(jnp.int32, (CHUNK, LANES), 0)
    lane_axis = lax.broadcasted_iota(jnp.int32, (CHUNK, LANES), 1)

    def segment_of(position):
        result = jnp.int32(0)
        for edge in range(SPG):
            result = result + (position >= bounds_ref[edge]).astype(jnp.int32)
        return result

    row_seg = segment_of(row_axis + first_row)
    lane_seg = segment_of(lane_axis + first_row)
    seg_in = segment_of(jnp.maximum(first_row - 1, 0))
    seg_last = segment_of(first_row + CHUNK - 1)
    same = row_seg == lane_seg
    lower = row_axis >= lane_axis
    carried = (row_seg == seg_in).astype(jnp.float32)
    tail = (row_seg == seg_last).astype(jnp.float32)
    keep = (seg_last == seg_in).astype(jnp.float32)

    def group_of(index):
        return (index >= R).astype(jnp.int32) + (index >= R + NS).astype(jnp.int32)

    group_row, group_lane = group_of(row_axis), group_of(lane_axis)
    group_mean = jnp.where(
        group_row == group_lane, jnp.where(group_lane == 0, 1.0 / R, 1.0 / NS), 0.0
    )
    gains = params_ref[0:1, :]
    step_b = params_ref[1:2, :]
    rate = jnp.exp(params_ref[2:3, :])
    scale = lax.rsqrt(exact_dot(proj * proj, group_mean) + EPSILON)
    unit = proj * scale
    normed = unit * gains
    step_pre = exact_dot(normed, step_w) + step_b
    step_size = jnp.maximum(step_pre, 0.0) + jnp.log1p(jnp.exp(-jnp.abs(step_pre)))
    log_decay = -step_size * rate
    cumulative = exact_dot(lower.astype(jnp.float32), log_decay)
    low_lanes = lane_axis < NS
    input_b = jnp.where(low_lanes, pltpu.roll(normed, LANES - R, 1), 0.0)
    output_c = jnp.where(low_lanes, pltpu.roll(normed, LANES - R - NS, 1), 0.0)
    last = cumulative[CHUNK - 1 : CHUNK, :]
    return dict(
        lane_axis=lane_axis,
        same=same,
        lower=lower,
        group_mean=group_mean,
        gains=gains,
        rate=rate,
        scale=scale,
        unit=unit,
        normed=normed,
        step_pre=step_pre,
        step_size=step_size,
        log_decay=log_decay,
        cumulative=cumulative,
        input_b=input_b,
        output_c=output_c,
        head_in=jnp.exp(cumulative) * carried,
        head_out=jnp.exp(last - cumulative) * tail,
        head_keep=jnp.exp(last) * keep,
    )


def scan_forward_kernel(
    head_width,
    bounds_ref,
    proj_ref,
    conv_ref,
    gate_ref,
    params_ref,
    step_w_ref,
    skip_ref,
    expand_ref,
    gated_ref,
    scanned_ref,
    states_ref,
    state_ref,
):
    chunk_index = pl.program_id(0)

    @pl.when(chunk_index == 0)
    def _():
        state_ref[...] = jnp.zeros_like(state_ref)

    state = state_ref[...]
    states_ref[0] = state
    prep = chunk_setup(bounds_ref, chunk_index, proj_ref[...], params_ref, step_w_ref[...])
    expand = expand_ref[...]
    channel_count = conv_ref.shape[1]
    conv_in = conv_ref[...].astype(jnp.float32)
    weighted = split_dot(prep["step_size"], expand, 0, 2) * conv_in
    weighted_parts = [weighted.astype(jnp.bfloat16)]
    weighted_parts.append((weighted - weighted_parts[0].astype(jnp.float32)).astype(jnp.bfloat16))
    tail_values = split_dot(prep["head_out"], expand, 0, 2) * weighted
    keep = split_dot(jnp.broadcast_to(prep["head_keep"], (8, LANES)), expand, 0, 2)[0:1, :]
    b_rows = prep["input_b"].T[0:NS, :]
    state_ref[...] = keep * state + fine_dot(b_rows, tail_values)
    scores = exact_dot(prep["output_c"], prep["input_b"], 1, 1)
    scores = jnp.where(prep["same"] & prep["lower"], scores, 0.0)
    from_state = split_dot(prep["head_in"], expand, 0, 2) * fine_dot(
        prep["output_c"][:, 0:NS], state
    )
    cumulative = prep["cumulative"]
    cumulative_t = cumulative.T
    lane_axis = prep["lane_axis"]
    for tile in range(channel_count // LANES):
        columns = slice(tile * LANES, (tile + 1) * LANES)
        parts = [part[:, columns] for part in weighted_parts]
        mixing, masked = [], [[], []]
        for head, low, high in tile_heads(tile, head_width, channel_count):
            spread = cumulative[:, head : head + 1] - cumulative_t[head : head + 1, :]
            mixing.append((scores * jnp.exp(jnp.minimum(spread, 0.0))).astype(jnp.bfloat16))
            own = (lane_axis >= low) & (lane_axis < high)
            for part, kept in zip(parts, masked):
                kept.append(jnp.where(own, part, jnp.zeros_like(part)))
        mixing = jnp.concatenate(mixing, axis=1)
        inside = mixed_dot(mixing, jnp.concatenate(masked[0], axis=0)) + mixed_dot(
            mixing, jnp.concatenate(masked[1], axis=0)
        )
        scanned = inside + from_state[:, columns]
        scanned_ref[:, columns] = scanned
        gate = gate_ref[:, columns].astype(jnp.float32)
        mixed_out = scanned + skip_ref[:, columns] * conv_in[:, columns]
        gated_ref[:, columns] = (mixed_out * (gate / (1.0 + jnp.exp(-gate)))).astype(jnp.bfloat16)


def scan_backward_kernel(
    head_width,
    bounds_ref,
    upstream_ref,
    proj_ref,
    conv_ref,
    gate_ref,
    scanned_ref,
    states_ref,
    params_ref,
    step_w_ref,
    skip_ref,
    expand_ref,
    proj_grad_ref,
    conv_grad_ref,
    gate_grad_ref,
    step_w_grad_ref,
    rows_grad_ref,
    skip_grad_ref,
    state_grad_ref,
):
    step = pl.program_id(0)
    chunk_index = pl.num_programs(0) - 1 - step

    @pl.when(step == 0)
    def _():
        state_grad_ref[...] = jnp.zeros_like(state_grad_ref)
        step_w_grad_ref[...] = jnp.zeros_like(step_w_grad_ref)
        rows_grad_ref[...] = jnp.zeros_like(rows_grad_ref)
        skip_grad_ref[...] = jnp.zeros_like(skip_grad_ref)

    state = states_ref[0]
    state_grad = state_grad_ref[...]
    step_w = step_w_ref[...]
    prep = chunk_setup(bounds_ref, chunk_index, proj_ref[...], params_ref, step_w)
    expand = expand_ref[...]
    channel_count = conv_ref.shape[1]
    conv_in = conv_ref[...].astype(jnp.float32)
    step_wide = split_dot(prep["step_size"], expand, 0, 2)
    weighted = step_wide * conv_in
    weighted_low = weighted.astype(jnp.bfloat16)
    out_wide = split_dot(prep["head_out"], expand, 0, 2)
    in_wide = split_dot(prep["head_in"], expand, 0, 2)
    keep = split_dot(jnp.broadcast_to(prep["head_keep"], (8, LANES)), expand, 0, 2)[0:1, :]
    tail_values = out_wide * weighted
    b_rows = prep["input_b"].T[0:NS, :]
    c_rows = prep["output_c"].T[0:NS, :]
    state_out = keep * state + fine_dot(b_rows, tail_values)

    gate = gate_ref[...].astype(jnp.float32)
    upstream = upstream_ref[...].astype(jnp.float32)
    scanned = scanned_ref[...]
    logistic = 1.0 / (1.0 + jnp.exp(-gate))
    mixed_grad = upstream * (gate * logistic)
    mixed_out = scanned + skip_ref[...] * conv_in
    gate_grad_ref[...] = (
        upstream * mixed_out * (logistic * (1.0 + gate * (1.0 - logistic)))
    ).astype(jnp.bfloat16)
    skip_grad_ref[0:1, :] += jnp.sum(mixed_grad * conv_in, axis=0, keepdims=True)
    grad_low = mixed_grad.astype(jnp.bfloat16)
    grad_round = grad_low.astype(jnp.float32)

    pad_rows = jnp.zeros((LANES - NS, channel_count), jnp.float32)
    state_tall = jnp.concatenate([state, pad_rows], axis=0)
    state_grad_tall = jnp.concatenate([state_grad, pad_rows], axis=0)
    from_in = in_wide * grad_round
    c_grad = mixed_dot(from_in, state_tall, 1, 1)
    b_grad = mixed_dot(tail_values, state_grad_tall, 1, 1)
    weighted_grad = out_wide * fine_dot(prep["input_b"][:, 0:NS], state_grad)
    state_grad_ref[...] = keep * state_grad + fine_dot(c_rows, from_in)

    row_axis = lax.broadcasted_iota(jnp.int32, (CHUNK, LANES), 0)
    upper = prep["same"] & (row_axis <= prep["lane_axis"])
    scores_t = jnp.where(upper, exact_dot(prep["input_b"], prep["output_c"], 1, 1), 0.0)
    cumulative = prep["cumulative"]
    cumulative_t = cumulative.T
    lane_axis = prep["lane_axis"]
    scores_grad = jnp.zeros((CHUNK, LANES), jnp.float32)
    inside_grads = []
    for tile in range(channel_count // LANES):
        columns = slice(tile * LANES, (tile + 1) * LANES)
        values = weighted_low[:, columns]
        grads = grad_low[:, columns]
        mixing, masked_values, masked_grads, decays = [], [], [], []
        for head, low, high in tile_heads(tile, head_width, channel_count):
            spread = cumulative_t[head : head + 1, :] - cumulative[:, head : head + 1]
            decay = jnp.exp(jnp.minimum(spread, 0.0))
            decays.append(decay)
            mixing.append((scores_t * decay).astype(jnp.bfloat16))
            own = (lane_axis >= low) & (lane_axis < high)
            masked_values.append(jnp.where(own, values, jnp.zeros_like(values)))
            masked_grads.append(jnp.where(own, grads, jnp.zeros_like(grads)))
        pair_grads = mixed_dot(jnp.concatenate(masked_values, axis=0), grads, 1, 1)
        for place, decay in enumerate(decays):
            scores_grad = scores_grad + decay * pair_grads[place * CHUNK : (place + 1) * CHUNK, :]
        inside_grads.append(
            mixed_dot(jnp.concatenate(mixing, axis=1), jnp.concatenate(masked_grads, axis=0))
        )
    weighted_grad = weighted_grad + jnp.concatenate(inside_grads, axis=1)
    scores_grad = jnp.where(upper, scores_grad, 0.0)
    b_grad = b_grad + mixed_dot(scores_grad, prep["output_c"])
    c_grad = c_grad + mixed_dot(scores_grad.T, prep["input_b"])
    conv_grad_ref[...] = mixed_grad * skip_ref[...] + weighted_grad * step_wide
    spread_grad = split_dot(
        grad_round * scanned - weighted * weighted_grad, expand, 1, 3
    )
    edge = jnp.broadcast_to(
        jnp.sum(state_out * state_grad, axis=0, keepdims=True), (8, channel_count)
    )
    edge_grad = split_dot(edge, expand, 1, 3)[0:1, :]
    spread_grad = spread_grad + jnp.where(row_axis == CHUNK - 1, edge_grad, 0.0)
    decay_grad = exact_dot((row_axis <= lane_axis).astype(jnp.float32), spread_grad)
    step_grad = split_dot(weighted_grad * conv_in, expand, 1, 2) - decay_grad * prep["rate"]
    step_pre = prep["step_pre"]
    pre_grad = step_grad / (1.0 + jnp.exp(-step_pre))
    step_w_grad_ref[...] += exact_dot(prep["normed"].T, pre_grad)
    normed_grad = (
        exact_dot(pre_grad, step_w, 1, 1)
        + pltpu.roll(b_grad, R, 1)
        + pltpu.roll(c_grad, R + NS, 1)
    )
    unit = prep["unit"]
    rows_grad_ref[0:1, :] += jnp.sum(normed_grad * unit, axis=0, keepdims=True)
    rows_grad_ref[1:2, :] += jnp.sum(pre_grad, axis=0, keepdims=True)
    rows_grad_ref[2:3, :] += jnp.sum(decay_grad * prep["log_decay"], axis=0, keepdims=True)
    unit_grad = normed_grad * prep["gains"]
    along = exact_dot(unit_grad * unit, prep["group_mean"], 1, 1)
    proj_grad_ref[...] = prep["scale"] * (unit_grad - unit * along)


def scan_operands(step_weight, step_bias, log_rate, skip_gain, proj_gains, head_width):
    head_count = step_bias.shape[0]
    channel_count = skip_gain.shape[0]

    def lane_row(values):
        return jnp.pad(values.astype(jnp.float32), (0, LANES - values.shape[0]))[None, :]

    params = jnp.concatenate(
        [
            lane_row(proj_gains),
            lane_row(step_bias),
            lane_row(log_rate),
            jnp.zeros((5, LANES), jnp.float32),
        ],
        axis=0,
    )
    step_w = jnp.pad(
        step_weight.astype(jnp.float32), ((0, LANES - R), (0, LANES - head_count))
    )
    skip = skip_gain.astype(jnp.float32)[None, :]
    owner = lax.broadcasted_iota(jnp.int32, (LANES, channel_count), 1) // head_width
    head = lax.broadcasted_iota(jnp.int32, (LANES, channel_count), 0)
    return params, step_w, skip, (owner == head).astype(jnp.bfloat16)


def whole(shape):
    return pl.BlockSpec(shape, lambda i, *_: (0,) * len(shape))


def scan_forward(bounds, projected, conv_out, gate_pre, operands, head_width):
    params, step_w, skip, expand = operands
    rows, channels = conv_out.shape
    chunks = rows // CHUNK

    def chunk_rows(width):
        return pl.BlockSpec((CHUNK, width), lambda i, *_: (i, 0))

    return pl.pallas_call(
        functools.partial(scan_forward_kernel, head_width),
        out_shape=(
            jax.ShapeDtypeStruct((rows, channels), jnp.bfloat16),
            jax.ShapeDtypeStruct((rows, channels), jnp.float32),
            jax.ShapeDtypeStruct((chunks, NS, channels), jnp.float32),
        ),
        grid_spec=pltpu.PrefetchScalarGridSpec(
            num_scalar_prefetch=1,
            grid=(chunks,),
            in_specs=[
                chunk_rows(LANES),
                chunk_rows(channels),
                chunk_rows(channels),
                whole(params.shape),
                whole(step_w.shape),
                whole(skip.shape),
                whole(expand.shape),
            ],
            out_specs=[
                chunk_rows(channels),
                chunk_rows(channels),
                pl.BlockSpec((1, NS, channels), lambda i, *_: (i, 0, 0)),
            ],
            scratch_shapes=[pltpu.VMEM((NS, channels), jnp.float32)],
        ),
        cost_estimate=pl.CostEstimate(
            flops=100_000_000, bytes_accessed=100_000, transcendentals=0
        ),
        name="scan_forward",
    )(bounds, projected, conv_out, gate_pre, params, step_w, skip, expand)


def scan_backward(bounds, upstream, projected, conv_out, gate_pre, scanned, states, operands, head_width):
    params, step_w, skip, expand = operands
    rows, channels = conv_out.shape
    chunks = rows // CHUNK

    def chunk_rows(width):
        return pl.BlockSpec((CHUNK, width), lambda i, *_: (chunks - 1 - i, 0))

    return pl.pallas_call(
        functools.partial(scan_backward_kernel, head_width),
        out_shape=(
            jax.ShapeDtypeStruct((rows, LANES), jnp.float32),
            jax.ShapeDtypeStruct((rows, channels), jnp.float32),
            jax.ShapeDtypeStruct((rows, channels), jnp.bfloat16),
            jax.ShapeDtypeStruct((LANES, LANES), jnp.float32),
            jax.ShapeDtypeStruct((8, LANES), jnp.float32),
            jax.ShapeDtypeStruct((8, channels), jnp.float32),
        ),
        grid_spec=pltpu.PrefetchScalarGridSpec(
            num_scalar_prefetch=1,
            grid=(chunks,),
            in_specs=[
                chunk_rows(channels),
                chunk_rows(LANES),
                chunk_rows(channels),
                chunk_rows(channels),
                chunk_rows(channels),
                pl.BlockSpec((1, NS, channels), lambda i, *_: (chunks - 1 - i, 0, 0)),
                whole(params.shape),
                whole(step_w.shape),
                whole(skip.shape),
                whole(expand.shape),
            ],
            out_specs=[
                chunk_rows(LANES),
                chunk_rows(channels),
                chunk_rows(channels),
                whole((LANES, LANES)),
                whole((8, LANES)),
                whole((8, channels)),
            ],
            scratch_shapes=[pltpu.VMEM((NS, channels), jnp.float32)],
        ),
        cost_estimate=pl.CostEstimate(
            flops=100_000_000, bytes_accessed=100_000, transcendentals=0
        ),
        name="scan_backward",
    )(bounds, upstream, projected, conv_out, gate_pre, scanned, states, params, step_w, skip, expand)


PLACES = (0, 2, 1, 3)


def swap_pairs(size, flip):
    return [(index, index ^ flip) for index in range(size)]


class Wires:
    def __init__(self, dp_size, tensor_size):
        self.dp_size = dp_size
        self.tensor_size = tensor_size
        self.staged = tensor_size == 4 and dp_size == 8
        self.group = lax.axis_index("dp")
        self.lane = lax.axis_index("tensor")
        self.outer = self.group // 2
        self.inner = self.group % 2
        self.turn = jnp.bitwise_xor(self.lane, self.outer)

    def over_tensor(self, values, flip):
        return lax.ppermute(values, "tensor", swap_pairs(self.tensor_size, flip))

    def over_dp(self, values, flip):
        return lax.ppermute(values, "dp", swap_pairs(self.dp_size, flip))

    def place_of(self, distance):
        block = jnp.bitwise_xor(self.turn, distance)
        return (block & 1) * 2 + (block >> 1)


    def gather_features(self, values, until=None, deadline=None):
        if not self.staged:
            rows = lax.all_gather(values, "tensor", axis=1, tiled=True)
            return rows if deadline is None else (rows, deadline)
        across = self.over_tensor(values, 2)
        beside = self.over_tensor(values, 1)
        diagonal = self.over_tensor(across if until is None else after(across, until), 1)
        if deadline is not None:
            across, beside, diagonal, deadline = lax.optimization_barrier(
                (across, beside, diagonal, deadline)
            )
        rows = jnp.concatenate([values, across, beside, diagonal], axis=1)
        return rows if deadline is None else (rows, deadline)

    def sum_features(self, project, start=None, until=None, across_start=None):
        width = D // self.tensor_size
        if not self.staged:
            return lax.psum_scatter(
                project(slice(0, D)), "tensor", scatter_dimension=1, tiled=True
            )
        sent = project(slice(2 * width, 4 * width)).astype(jnp.bfloat16)
        if start is not None:
            sent = after(sent, start)
        kept = project(slice(0, 2 * width))
        total = kept + self.over_tensor(sent, 1).astype(jnp.float32)
        passed = total[:, width:].astype(jnp.bfloat16)
        if across_start is not None:
            passed = after(passed, across_start)
        across = self.over_tensor(passed, 2)
        if until is not None:
            across = after(across, until)
        return total[:, :width] + across.astype(jnp.float32)

    def sum_small(self, values):
        if not self.staged:
            return lax.psum(values, "tensor")
        values = values + self.over_tensor(values, 1)
        return values + self.over_tensor(values, 2)

    def sum_rows(self, values, wire):
        if not self.staged:
            return lax.psum(values.astype(wire), "tensor").astype(jnp.float32)
        half = values.shape[0] // 2
        core = self.lane % 2
        kept = lax.dynamic_slice_in_dim(values, core * half, half)
        sent = lax.dynamic_slice_in_dim(values, (1 - core) * half, half)
        total = kept + self.over_tensor(sent.astype(wire), 1).astype(jnp.float32)
        total = total + self.over_tensor(total.astype(wire), 2).astype(jnp.float32)
        other = self.over_tensor(total.astype(wire), 1).astype(jnp.float32)
        total = total.astype(wire).astype(jnp.float32)
        first = jnp.where(core == 0, total, other)
        second = jnp.where(core == 0, other, total)
        return jnp.concatenate([first, second], axis=0)


    def block_order(self):
        return jnp.stack([jnp.bitwise_xor(self.lane, place) for place in PLACES]).astype(jnp.int32)

    def gather_whole(self, shard, widths):
        whole_rows = lax.all_gather(shard, "dp", axis=0, tiled=True)
        if not self.staged:
            return split_columns(whole_rows, widths)
        return move_blocks(self.block_order(), whole_rows, widths)

    def sum_whole(self, grads, earlier=None):
        widths = [grad.shape[1] for grad in grads]
        if self.staged:
            joined = restore_blocks(self.block_order(), grads)
        else:
            joined = jnp.concatenate(grads, axis=1)
        if earlier is not None:
            joined = after(joined, earlier)
        total = lax.psum_scatter(joined, "dp", scatter_dimension=0, tiled=True)
        return [part.astype(jnp.float32) for part in split_columns(total, widths)], joined


    def sum_across(self, grad):
        blocks = grad.reshape(4, 2, D // 8, grad.shape[1])
        sent = lax.dynamic_index_in_dim(blocks, 1 - self.inner, 1, keepdims=False)
        kept = lax.dynamic_index_in_dim(blocks, self.inner, 1, keepdims=False)
        return kept, self.over_dp(sent, 1)

    def sum_far(self, across, marker):
        kept, got = across
        total = (kept.astype(jnp.float32) + after(got, marker).astype(jnp.float32)).astype(
            jnp.bfloat16
        )

        def pair(near, far):
            return [
                lax.dynamic_index_in_dim(total, self.place_of(place), 0, keepdims=False)
                for place in (near, far)
            ]

        return pair(0, 1), self.over_dp(jnp.concatenate(pair(2, 3), axis=0), 4)

    def sum_near(self, far, marker):
        (own, near), got = far
        got = after(got, marker).astype(jnp.float32)
        rows = own.shape[0]
        sent = (near.astype(jnp.float32) + got[rows:]).astype(jnp.bfloat16)
        return own.astype(jnp.float32) + got[:rows], self.over_dp(sent, 2)

    def sum_end(self, near):
        total, got = near
        return total + got.astype(jnp.float32)

    def exchange(self, blocks):
        return lax.all_to_all(blocks, "dp", split_axis=0, concat_axis=0, tiled=True)


def split_columns(values, widths):
    parts, start = [], 0
    for width in widths:
        parts.append(values[:, start : start + width])
        start += width
    return parts


def move_kernel(order_ref, whole_ref, *outs):
    start = 0
    for out in outs:
        width = out.shape[1]
        out[...] = whole_ref[:, start : start + width]
        start += width


def move_blocks(order, gathered, widths):
    rows, width = gathered.shape
    block = rows // 4
    return pl.pallas_call(
        move_kernel,
        out_shape=[jax.ShapeDtypeStruct((rows, part), jnp.bfloat16) for part in widths],
        grid_spec=pltpu.PrefetchScalarGridSpec(
            num_scalar_prefetch=1,
            grid=(4,),
            in_specs=[pl.BlockSpec((block, width), lambda i, order_ref: (order_ref[i], 0))],
            out_specs=[
                pl.BlockSpec((block, part), lambda i, order_ref: (i, 0)) for part in widths
            ],
        ),
        cost_estimate=pl.CostEstimate(
            flops=0, bytes_accessed=4 * rows * width, transcendentals=0
        ),
        name="move_blocks",
    )(order, gathered)


def restore_kernel(order_ref, *refs):
    out, start = refs[-1], 0
    for ref in refs[:-1]:
        width = ref.shape[1]
        out[:, start : start + width] = ref[...]
        start += width


def restore_blocks(order, grads):
    rows = grads[0].shape[0]
    block = rows // 4
    width = sum(grad.shape[1] for grad in grads)
    return pl.pallas_call(
        restore_kernel,
        out_shape=jax.ShapeDtypeStruct((rows, width), jnp.bfloat16),
        grid_spec=pltpu.PrefetchScalarGridSpec(
            num_scalar_prefetch=1,
            grid=(4,),
            in_specs=[
                pl.BlockSpec((block, grad.shape[1]), lambda i, order_ref: (i, 0))
                for grad in grads
            ],
            out_specs=pl.BlockSpec((block, width), lambda i, order_ref: (order_ref[i], 0)),
        ),
        cost_estimate=pl.CostEstimate(
            flops=0, bytes_accessed=4 * rows * width, transcendentals=0
        ),
        name="restore_blocks",
    )(order, *grads)


def pack_rows(parts, lanes):
    blocks = parts[0].shape[0]
    flat = jnp.concatenate([part.reshape(blocks, -1) for part in parts], axis=1)
    size = flat.shape[1]
    rows = -(-size // (16 * lanes)) * 16
    flat = jnp.pad(flat, ((0, 0), (0, rows * lanes - size)))
    return flat.reshape(blocks, rows, lanes)


def unpack_rows(packed, shapes):
    blocks = packed.shape[0]
    flat = packed.reshape(blocks, -1)
    parts, start = [], 0
    for shape in shapes:
        size = 1
        for extent in shape:
            size *= extent
        parts.append(flat[:, start : start + size].reshape((blocks,) + shape))
        start += size
    return parts


def after(values, earlier):
    return lax.optimization_barrier((values, earlier))[0]


def row_scale(wires, values):
    mean_square = wires.sum_small(jnp.sum(values * values, axis=1).reshape(-1, LANES)) / D
    return lax.rsqrt(mean_square + EPSILON).reshape(-1)


def norm_back(wires, values, inverse, gain, upstream):
    normed = values * inverse[:, None]
    gain_grad = jnp.sum(upstream * normed, axis=0)
    scaled = upstream * gain
    along = jnp.sum(scaled * normed, axis=1).reshape(-1, LANES)
    along = wires.sum_small(along).reshape(-1) / D
    return inverse[:, None] * (scaled - normed * along[:, None]), gain_grad


def per_device(
    dp_size,
    tensor_size,
    tokens,
    out_grad,
    lengths,
    deal,
    mixer_gain,
    inner_weight,
    gate_weight,
    conv_taps,
    conv_bias,
    proj_weight,
    proj_gains,
    step_weight,
    step_bias,
    log_rate,
    skip_gain,
    out_weight,
    ffn_gain,
    ffn_gate,
    ffn_up,
    ffn_down,
):
    wires = Wires(dp_size, tensor_size)
    group = wires.group
    bf16, f32 = jnp.bfloat16, jnp.float32

    packed_lengths = lengths[deal]
    group_lengths = lax.dynamic_slice_in_dim(packed_lengths, group * SPG, SPG)
    starts = jnp.cumsum(group_lengths) - group_lengths
    filled = jnp.sum(group_lengths)
    bounds = jnp.concatenate([starts[1:], filled[None]]).astype(jnp.int32)
    row_ids = jnp.arange(GCAP, dtype=jnp.int32)
    live_rows = row_ids < filled
    segment = jnp.sum((row_ids[:, None] >= bounds[None, :]).astype(jnp.int32), axis=1)
    slot = jnp.minimum(segment, SPG - 1)
    position = row_ids - jnp.where(slot == 0, 0, starts[slot])
    span = LMAX // dp_size

    small_parts = (
        proj_weight,
        mixer_gain,
        conv_taps,
        conv_bias,
        proj_gains,
        step_weight,
        step_bias,
        log_rate,
        skip_gain,
        ffn_gain,
    )
    small_shapes = [part.shape for part in small_parts]
    small = pack_rows([part[None] for part in small_parts], tokens.shape[2])
    small_rows = small.shape[1]
    order = jnp.arange(dp_size, dtype=jnp.int32)
    if wires.staged:
        order = jnp.bitwise_xor(order, group)
    dealt = tokens[deal.reshape(dp_size, SPG)[order].reshape(-1)].reshape(dp_size, SPG * span, -1)
    sent = jnp.concatenate([dealt, jnp.broadcast_to(small, (dp_size,) + small.shape[1:])], axis=1)
    if wires.staged:
        arrived = jnp.stack(
            [sent[0]] + [wires.over_dp(sent[flip], flip) for flip in range(1, dp_size)]
        )
    else:
        arrived = wires.exchange(sent)
    flat_rows = arrived.reshape(dp_size * (SPG * span + small_rows), -1)
    origin = position // span
    if wires.staged:
        origin = jnp.bitwise_xor(origin, group)
    source_rows = origin * (SPG * span + small_rows) + slot * span + position % span
    source_rows = jnp.where(live_rows, source_rows, 0)
    packed = jnp.where(live_rows[:, None], flat_rows[source_rows], 0.0).astype(f32)
    small = unpack_rows(arrived[:, SPG * span :][order], small_shapes)

    def along_last(part):
        return jnp.moveaxis(part, 0, -2).reshape(part.shape[1:-1] + (-1,))

    proj_all = small[0].reshape(-1, small[0].shape[-1])
    gain_all, taps_all, bias_all, gains_all, step_w_all, step_b_all, rate_all, skip_all, ffn_gain_all = [
        along_last(part).astype(f32) for part in small[1:]
    ]

    staged = wires.staged
    in_width, out_width = [inner_weight.shape[1]], [out_weight.shape[0]]
    down_width, ffn_widths = [ffn_down.shape[0]], [ffn_gate.shape[1], ffn_up.shape[1]]
    inner_all, gate_all, out_all = wires.gather_whole(
        jnp.concatenate([inner_weight, gate_weight, out_weight.T], axis=1), in_width * 2 + out_width
    )

    inverse_in = row_scale(wires, packed)
    mixer_rows = wires.gather_features((packed * inverse_in[:, None] * gain_all).astype(bf16))
    ffn_gate_all, ffn_up_all, ffn_down_all = wires.gather_whole(
        after(jnp.concatenate([ffn_gate, ffn_up, ffn_down.T], axis=1), (inner_all, mixer_rows)),
        ffn_widths + down_width,
    )
    inner_pre = contract(mixer_rows, inner_all, 1, 0)
    conv_out = conv_silu(inner_pre, taps_all, bias_all, segment).astype(bf16)
    proj_terms = contract(conv_out, proj_all, 1, 0)
    projected = wires.sum_rows(proj_terms, f32)
    gate_pre = contract(mixer_rows, gate_all, 1, 0)
    operands = scan_operands(step_w_all, step_b_all, rate_all, skip_all, gains_all, HEAD_WIDTH)
    out_cot = jnp.where(live_rows[:, None], out_grad, 0.0).astype(bf16)
    gated, scanned, states = scan_forward(
        bounds, projected, conv_out, gate_pre, operands, HEAD_WIDTH
    )
    cot_rows, gated = wires.gather_features(after(out_cot, proj_terms), deadline=gated)
    residual = packed + wires.sum_features(lambda rows: contract(gated, out_all[rows], 1, 1))

    inverse_mid = row_scale(wires, residual)
    ffn_rows = wires.gather_features((residual * inverse_mid[:, None] * ffn_gain_all).astype(bf16), ffn_gate_all)
    gate_ffn = contract(ffn_rows, ffn_gate_all, 1, 0)
    up_ffn = contract(ffn_rows, ffn_up_all, 1, 0)
    logistic = jax.nn.sigmoid(gate_ffn)
    activated = gate_ffn * logistic
    hidden = (activated * up_ffn).astype(bf16)

    hidden_grad = contract(cot_rows, ffn_down_all, 1, 0)
    gate_grad = (hidden_grad * up_ffn * logistic * (1.0 + gate_ffn * (1.0 - logistic))).astype(bf16)
    up_grad = (hidden_grad * activated).astype(bf16)
    ffn_gate_terms = contract(ffn_rows, gate_grad, 0, 0).astype(bf16)
    ffn_up_terms = contract(ffn_rows, up_grad, 0, 0).astype(bf16)
    down_terms = contract(cot_rows, hidden, 0, 0).astype(bf16)
    (ffn_down_grad, ffn_gate_grad, ffn_up_grad), sums_ready = wires.sum_whole(
        [down_terms, ffn_gate_terms, ffn_up_terms]
    )
    mid_grad = wires.sum_features(
        lambda rows: contract(gate_grad, ffn_gate_all[rows], 1, 1)
        + contract(up_grad, ffn_up_all[rows], 1, 1),
        until=sums_ready,
    )
    mid_back, ffn_gain_grad = norm_back(wires, residual, inverse_mid, ffn_gain_all, mid_grad)
    residual_grad = out_cot.astype(f32) + mid_back
    branch = residual_grad.astype(bf16)
    branch_rows = wires.gather_features(branch)
    gated_grad = contract(branch_rows, out_all, 1, 0)
    final_rows = residual + wires.sum_features(
        lambda rows: contract(hidden, ffn_down_all[rows], 1, 1), start=branch_rows
    )
    out_terms = contract(branch_rows, gated, 0, 0).astype(bf16)
    if staged:
        out_across = wires.sum_across(out_terms)
        gated_grad = after(gated_grad, out_across[0])
    else:
        (out_weight_grad,), unused_sums = wires.sum_whole([out_terms])
    proj_part, conv_core_grad, gate_low, step_w_part, row_parts, skip_part = scan_backward(
        bounds, gated_grad, projected, conv_out, gate_pre, scanned, states, operands, HEAD_WIDTH
    )
    gate_terms = contract(after(mixer_rows, proj_part), gate_low, 0, 0).astype(bf16)
    if staged:
        proj_part, final_rows = lax.optimization_barrier((proj_part, final_rows))
    output = jnp.where(live_rows[:, None], final_rows, 0.0).astype(bf16)
    if staged:
        out_far = wires.sum_far(out_across, proj_part)
        proj_part = after(proj_part, out_far[0])
    head_count = step_b_all.shape[0]
    gains_grad = wires.sum_small(row_parts)[0]
    proj_low = wires.sum_rows(proj_part, bf16).astype(bf16)
    conv_grad = conv_core_grad + contract(proj_low, proj_all, 1, 1)
    proj_weight_grad = contract(conv_out, proj_low, 0, 0)

    def conv_piece(inner_in, taps_in, bias_in):
        return conv_silu(inner_in, taps_in, bias_in, segment)

    unused_conv, conv_pull = jax.vjp(conv_piece, inner_pre, taps_all, bias_all)
    inner_grad, taps_grad, bias_grad = conv_pull(conv_grad)
    inner_low = inner_grad.astype(bf16)
    inner_terms = contract(mixer_rows, inner_low, 0, 0).astype(bf16)
    earlier = ffn_gate_grad
    if staged:
        out_near = wires.sum_near(out_far, inner_terms)
        earlier = (ffn_gate_grad, out_near[0])
    (inner_weight_grad, gate_weight_grad), last_joined = wires.sum_whole(
        [inner_terms, gate_terms], earlier
    )
    in_grad = wires.sum_features(
        lambda rows: contract(inner_low, inner_all[rows], 1, 1)
        + contract(gate_low, gate_all[rows], 1, 1),
        until=inner_terms,
    )
    in_back, mixer_gain_grad = norm_back(wires, packed, inverse_in, gain_all, in_grad)

    def by_index(part):
        split = part.reshape(part.shape[:-1] + (dp_size, part.shape[-1] // dp_size))
        return jnp.moveaxis(split, -2, 0)

    small_grads = pack_rows(
        [
            part.astype(bf16)
            for part in (
                proj_weight_grad.reshape(dp_size, -1, proj_weight_grad.shape[1]),
                by_index(mixer_gain_grad),
                by_index(taps_grad),
                by_index(bias_grad),
                by_index(gains_grad),
                by_index(step_w_part[:R, :head_count]),
                by_index(row_parts[1, :head_count]),
                by_index(row_parts[2, :head_count]),
                by_index(skip_part[0]),
                by_index(ffn_gain_grad),
            )
        ],
        tokens.shape[2],
    )

    grad_packed = (residual_grad + in_back).astype(bf16)
    slot_position = jnp.arange(LMAX, dtype=jnp.int32).reshape(dp_size, 1, span)
    slot_live = slot_position < group_lengths[None, :, None]
    slot_rows = jnp.where(slot_live, starts[None, :, None] + slot_position, 0).reshape(-1)
    leaving = jnp.where(slot_live.reshape(-1)[:, None], grad_packed[slot_rows], 0.0)
    leaving = leaving.reshape(dp_size, SPG * span, -1)
    if staged:
        out_weight_grad = wires.sum_end(out_near)
    returned = wires.exchange(jnp.concatenate([leaving, small_grads], axis=1))
    inverse_deal = jnp.zeros_like(deal).at[deal].set(
        jnp.arange(deal.shape[0], dtype=jnp.int32)
    )
    tokens_grad = returned[:, : SPG * span].reshape(dp_size * SPG, span, -1)[inverse_deal]
    (
        proj_weight_grad,
        mixer_gain_grad,
        taps_grad,
        bias_grad,
        gains_grad,
        step_w_grad,
        step_b_grad,
        rate_grad,
        skip_grad,
        ffn_gain_grad,
    ) = unpack_rows(
        jnp.sum(returned[:, SPG * span :].astype(f32), axis=0)[None], small_shapes
    )

    return (
        output,
        tokens_grad,
        mixer_gain_grad[0],
        inner_weight_grad,
        gate_weight_grad,
        taps_grad[0],
        bias_grad[0],
        proj_weight_grad[0],
        gains_grad[0],
        step_w_grad[0],
        step_b_grad[0],
        rate_grad[0],
        skip_grad[0],
        out_weight_grad.T,
        ffn_gain_grad[0],
        ffn_gate_grad,
        ffn_up_grad,
        ffn_down_grad.T,
    )


def solution(mesh):
    return jax.shard_map(
        functools.partial(per_device, mesh.shape["dp"], mesh.shape["tensor"]),
        mesh=mesh,
        in_specs=(
            P(None, "dp", "tensor"),
            P("dp", "tensor"),
            P(),
            P(),
            P(("tensor", "dp")),
            P("dp", "tensor"),
            P("dp", "tensor"),
            P(None, ("tensor", "dp")),
            P(("tensor", "dp")),
            P(("tensor", "dp"), None),
            P("dp"),
            P(None, ("tensor", "dp")),
            P(("tensor", "dp")),
            P(("tensor", "dp")),
            P(("tensor", "dp")),
            P("tensor", "dp"),
            P(("tensor", "dp")),
            P("dp", "tensor"),
            P("dp", "tensor"),
            P("tensor", "dp"),
        ),
        out_specs=(
            P("dp", "tensor"),
            P(None, "dp", "tensor"),
            P(("tensor", "dp")),
            P("dp", "tensor"),
            P("dp", "tensor"),
            P(None, ("tensor", "dp")),
            P(("tensor", "dp")),
            P(("tensor", "dp"), None),
            P("dp"),
            P(None, ("tensor", "dp")),
            P(("tensor", "dp")),
            P(("tensor", "dp")),
            P(("tensor", "dp")),
            P("tensor", "dp"),
            P(("tensor", "dp")),
            P("dp", "tensor"),
            P("dp", "tensor"),
            P("tensor", "dp"),
        ),
        check_vma=False,
    )
```

```python
import functools

import jax
import jax.numpy as jnp
from jax import lax
from jax.experimental import pallas as pl
from jax.experimental.pallas import tpu as pltpu
from jax.sharding import PartitionSpec as P

D = 1536
NS = 16
KC = 4
R = 96
LMAX = 1024
SPG = 2
GCAP = 1280
HEAD_WIDTH = 24


HIGHEST = lax.Precision.HIGHEST
EPSILON = 1e-06


def contract(left, right, left_dim, right_dim):
    return lax.dot_general(
        left, right, (((left_dim,), (right_dim,)), ((), ())), preferred_element_type=jnp.float32
    )


def conv_silu(inner_pre, conv_taps, conv_bias, segment):
    row_count = inner_pre.shape[0]
    running_sum = conv_bias + conv_taps[KC - 1] * inner_pre
    for offset in range(1, KC):
        earlier = jnp.concatenate(
            [
                jnp.zeros((offset, inner_pre.shape[1]), inner_pre.dtype),
                inner_pre[: row_count - offset],
            ],
            axis=0,
        )
        linked = jnp.concatenate(
            [jnp.zeros((offset,), jnp.bool_), segment[offset:] == segment[: row_count - offset]]
        )
        running_sum = running_sum + conv_taps[KC - 1 - offset] * jnp.where(
            linked[:, None], earlier, 0.0
        )
    return jax.nn.silu(running_sum)


LANES = 128
CHUNK = 128


def mixed_dot(left, right, left_dim=1, right_dim=0):
    return lax.dot_general(
        left.astype(jnp.bfloat16),
        right.astype(jnp.bfloat16),
        (((left_dim,), (right_dim,)), ((), ())),
        preferred_element_type=jnp.float32,
    )


def fine_dot(left, right, left_dim=1, right_dim=0):
    left_high, right_high = left.astype(jnp.bfloat16), right.astype(jnp.bfloat16)
    left_low = (left - left_high.astype(jnp.float32)).astype(jnp.bfloat16)
    right_low = (right - right_high.astype(jnp.float32)).astype(jnp.bfloat16)
    return (
        mixed_dot(left_high, right_high, left_dim, right_dim)
        + mixed_dot(left_high, right_low, left_dim, right_dim)
        + mixed_dot(left_low, right_high, left_dim, right_dim)
    )


def exact_dot(left, right, left_dim=1, right_dim=0):
    return lax.dot_general(
        left,
        right,
        (((left_dim,), (right_dim,)), ((), ())),
        precision=HIGHEST,
        preferred_element_type=jnp.float32,
    )


def split_dot(values, zero_one, right_dim, terms):
    total = None
    rest = values
    for term in range(terms):
        part = rest.astype(jnp.bfloat16)
        product = mixed_dot(part, zero_one, 1, right_dim)
        total = product if total is None else total + product
        if term + 1 < terms:
            rest = rest - part.astype(jnp.float32)
    return total


def tile_heads(tile, head_width, channel_count):
    first = tile * LANES
    heads = []
    for head in range(channel_count // head_width):
        low = max(head * head_width - first, 0)
        high = min((head + 1) * head_width - first, LANES)
        if low < high:
            heads.append((head, low, high))
    return heads


def chunk_setup(bounds_ref, chunk_index, proj, params_ref, step_w):
    first_row = chunk_index * CHUNK
    row_axis = lax.broadcasted_iota(jnp.int32, (CHUNK, LANES), 0)
    lane_axis = lax.broadcasted_iota(jnp.int32, (CHUNK, LANES), 1)

    def segment_of(position):
        result = jnp.int32(0)
        for edge in range(SPG):
            result = result + (position >= bounds_ref[edge]).astype(jnp.int32)
        return result

    row_seg = segment_of(row_axis + first_row)
    lane_seg = segment_of(lane_axis + first_row)
    seg_in = segment_of(jnp.maximum(first_row - 1, 0))
    seg_last = segment_of(first_row + CHUNK - 1)
    same = row_seg == lane_seg
    lower = row_axis >= lane_axis
    carried = (row_seg == seg_in).astype(jnp.float32)
    tail = (row_seg == seg_last).astype(jnp.float32)
    keep = (seg_last == seg_in).astype(jnp.float32)

    def group_of(index):
        return (index >= R).astype(jnp.int32) + (index >= R + NS).astype(jnp.int32)

    group_row, group_lane = group_of(row_axis), group_of(lane_axis)
    group_mean = jnp.where(
        group_row == group_lane, jnp.where(group_lane == 0, 1.0 / R, 1.0 / NS), 0.0
    )
    gains = params_ref[0:1, :]
    step_b = params_ref[1:2, :]
    rate = jnp.exp(params_ref[2:3, :])
    scale = lax.rsqrt(exact_dot(proj * proj, group_mean) + EPSILON)
    unit = proj * scale
    normed = unit * gains
    step_pre = exact_dot(normed, step_w) + step_b
    step_size = jnp.maximum(step_pre, 0.0) + jnp.log1p(jnp.exp(-jnp.abs(step_pre)))
    log_decay = -step_size * rate
    cumulative = exact_dot(lower.astype(jnp.float32), log_decay)
    low_lanes = lane_axis < NS
    input_b = jnp.where(low_lanes, pltpu.roll(normed, LANES - R, 1), 0.0)
    output_c = jnp.where(low_lanes, pltpu.roll(normed, LANES - R - NS, 1), 0.0)
    last = cumulative[CHUNK - 1 : CHUNK, :]
    return dict(
        lane_axis=lane_axis,
        same=same,
        lower=lower,
        group_mean=group_mean,
        gains=gains,
        rate=rate,
        scale=scale,
        unit=unit,
        normed=normed,
        step_pre=step_pre,
        step_size=step_size,
        log_decay=log_decay,
        cumulative=cumulative,
        input_b=input_b,
        output_c=output_c,
        head_in=jnp.exp(cumulative) * carried,
        head_out=jnp.exp(last - cumulative) * tail,
        head_keep=jnp.exp(last) * keep,
    )


def scan_forward_kernel(
    head_width,
    bounds_ref,
    proj_ref,
    conv_ref,
    gate_ref,
    params_ref,
    step_w_ref,
    skip_ref,
    expand_ref,
    gated_ref,
    scanned_ref,
    states_ref,
    state_ref,
):
    chunk_index = pl.program_id(0)

    @pl.when(chunk_index == 0)
    def _():
        state_ref[...] = jnp.zeros_like(state_ref)

    state = state_ref[...]
    states_ref[0] = state
    prep = chunk_setup(bounds_ref, chunk_index, proj_ref[...], params_ref, step_w_ref[...])
    expand = expand_ref[...]
    channel_count = conv_ref.shape[1]
    conv_in = conv_ref[...].astype(jnp.float32)
    weighted = split_dot(prep["step_size"], expand, 0, 2) * conv_in
    weighted_parts = [weighted.astype(jnp.bfloat16)]
    weighted_parts.append((weighted - weighted_parts[0].astype(jnp.float32)).astype(jnp.bfloat16))
    tail_values = split_dot(prep["head_out"], expand, 0, 2) * weighted
    keep = split_dot(jnp.broadcast_to(prep["head_keep"], (8, LANES)), expand, 0, 2)[0:1, :]
    b_rows = prep["input_b"].T[0:NS, :]
    state_ref[...] = keep * state + fine_dot(b_rows, tail_values)
    scores = exact_dot(prep["output_c"], prep["input_b"], 1, 1)
    scores = jnp.where(prep["same"] & prep["lower"], scores, 0.0)
    from_state = split_dot(prep["head_in"], expand, 0, 2) * fine_dot(
        prep["output_c"][:, 0:NS], state
    )
    cumulative = prep["cumulative"]
    cumulative_t = cumulative.T
    lane_axis = prep["lane_axis"]
    for tile in range(channel_count // LANES):
        columns = slice(tile * LANES, (tile + 1) * LANES)
        parts = [part[:, columns] for part in weighted_parts]
        mixing, masked = [], [[], []]
        for head, low, high in tile_heads(tile, head_width, channel_count):
            spread = cumulative[:, head : head + 1] - cumulative_t[head : head + 1, :]
            mixing.append((scores * jnp.exp(jnp.minimum(spread, 0.0))).astype(jnp.bfloat16))
            own = (lane_axis >= low) & (lane_axis < high)
            for part, kept in zip(parts, masked):
                kept.append(jnp.where(own, part, jnp.zeros_like(part)))
        mixing = jnp.concatenate(mixing, axis=1)
        inside = mixed_dot(mixing, jnp.concatenate(masked[0], axis=0)) + mixed_dot(
            mixing, jnp.concatenate(masked[1], axis=0)
        )
        scanned = inside + from_state[:, columns]
        scanned_ref[:, columns] = scanned
        gate = gate_ref[:, columns].astype(jnp.float32)
        mixed_out = scanned + skip_ref[:, columns] * conv_in[:, columns]
        gated_ref[:, columns] = (mixed_out * (gate / (1.0 + jnp.exp(-gate)))).astype(jnp.bfloat16)


def scan_backward_kernel(
    head_width,
    bounds_ref,
    upstream_ref,
    proj_ref,
    conv_ref,
    gate_ref,
    scanned_ref,
    states_ref,
    params_ref,
    step_w_ref,
    skip_ref,
    expand_ref,
    proj_grad_ref,
    conv_grad_ref,
    gate_grad_ref,
    step_w_grad_ref,
    rows_grad_ref,
    skip_grad_ref,
    state_grad_ref,
):
    step = pl.program_id(0)
    chunk_index = pl.num_programs(0) - 1 - step

    @pl.when(step == 0)
    def _():
        state_grad_ref[...] = jnp.zeros_like(state_grad_ref)
        step_w_grad_ref[...] = jnp.zeros_like(step_w_grad_ref)
        rows_grad_ref[...] = jnp.zeros_like(rows_grad_ref)
        skip_grad_ref[...] = jnp.zeros_like(skip_grad_ref)

    state = states_ref[0]
    state_grad = state_grad_ref[...]
    step_w = step_w_ref[...]
    prep = chunk_setup(bounds_ref, chunk_index, proj_ref[...], params_ref, step_w)
    expand = expand_ref[...]
    channel_count = conv_ref.shape[1]
    conv_in = conv_ref[...].astype(jnp.float32)
    step_wide = split_dot(prep["step_size"], expand, 0, 2)
    weighted = step_wide * conv_in
    weighted_low = weighted.astype(jnp.bfloat16)
    out_wide = split_dot(prep["head_out"], expand, 0, 2)
    in_wide = split_dot(prep["head_in"], expand, 0, 2)
    keep = split_dot(jnp.broadcast_to(prep["head_keep"], (8, LANES)), expand, 0, 2)[0:1, :]
    tail_values = out_wide * weighted
    b_rows = prep["input_b"].T[0:NS, :]
    c_rows = prep["output_c"].T[0:NS, :]
    state_out = keep * state + fine_dot(b_rows, tail_values)

    gate = gate_ref[...].astype(jnp.float32)
    upstream = upstream_ref[...].astype(jnp.float32)
    scanned = scanned_ref[...]
    logistic = 1.0 / (1.0 + jnp.exp(-gate))
    mixed_grad = upstream * (gate * logistic)
    mixed_out = scanned + skip_ref[...] * conv_in
    gate_grad_ref[...] = (
        upstream * mixed_out * (logistic * (1.0 + gate * (1.0 - logistic)))
    ).astype(jnp.bfloat16)
    skip_grad_ref[0:1, :] += jnp.sum(mixed_grad * conv_in, axis=0, keepdims=True)
    grad_low = mixed_grad.astype(jnp.bfloat16)
    grad_round = grad_low.astype(jnp.float32)

    pad_rows = jnp.zeros((LANES - NS, channel_count), jnp.float32)
    state_tall = jnp.concatenate([state, pad_rows], axis=0)
    state_grad_tall = jnp.concatenate([state_grad, pad_rows], axis=0)
    from_in = in_wide * grad_round
    c_grad = mixed_dot(from_in, state_tall, 1, 1)
    b_grad = mixed_dot(tail_values, state_grad_tall, 1, 1)
    weighted_grad = out_wide * fine_dot(prep["input_b"][:, 0:NS], state_grad)
    state_grad_ref[...] = keep * state_grad + fine_dot(c_rows, from_in)

    row_axis = lax.broadcasted_iota(jnp.int32, (CHUNK, LANES), 0)
    upper = prep["same"] & (row_axis <= prep["lane_axis"])
    scores_t = jnp.where(upper, exact_dot(prep["input_b"], prep["output_c"], 1, 1), 0.0)
    cumulative = prep["cumulative"]
    cumulative_t = cumulative.T
    lane_axis = prep["lane_axis"]
    scores_grad = jnp.zeros((CHUNK, LANES), jnp.float32)
    inside_grads = []
    for tile in range(channel_count // LANES):
        columns = slice(tile * LANES, (tile + 1) * LANES)
        values = weighted_low[:, columns]
        grads = grad_low[:, columns]
        mixing, masked_values, masked_grads, decays = [], [], [], []
        for head, low, high in tile_heads(tile, head_width, channel_count):
            spread = cumulative_t[head : head + 1, :] - cumulative[:, head : head + 1]
            decay = jnp.exp(jnp.minimum(spread, 0.0))
            decays.append(decay)
            mixing.append((scores_t * decay).astype(jnp.bfloat16))
            own = (lane_axis >= low) & (lane_axis < high)
            masked_values.append(jnp.where(own, values, jnp.zeros_like(values)))
            masked_grads.append(jnp.where(own, grads, jnp.zeros_like(grads)))
        pair_grads = mixed_dot(jnp.concatenate(masked_values, axis=0), grads, 1, 1)
        for place, decay in enumerate(decays):
            scores_grad = scores_grad + decay * pair_grads[place * CHUNK : (place + 1) * CHUNK, :]
        inside_grads.append(
            mixed_dot(jnp.concatenate(mixing, axis=1), jnp.concatenate(masked_grads, axis=0))
        )
    weighted_grad = weighted_grad + jnp.concatenate(inside_grads, axis=1)
    scores_grad = jnp.where(upper, scores_grad, 0.0)
    b_grad = b_grad + mixed_dot(scores_grad, prep["output_c"])
    c_grad = c_grad + mixed_dot(scores_grad.T, prep["input_b"])
    conv_grad_ref[...] = mixed_grad * skip_ref[...] + weighted_grad * step_wide
    spread_grad = split_dot(
        grad_round * scanned - weighted * weighted_grad, expand, 1, 3
    )
    edge = jnp.broadcast_to(
        jnp.sum(state_out * state_grad, axis=0, keepdims=True), (8, channel_count)
    )
    edge_grad = split_dot(edge, expand, 1, 3)[0:1, :]
    spread_grad = spread_grad + jnp.where(row_axis == CHUNK - 1, edge_grad, 0.0)
    decay_grad = exact_dot((row_axis <= lane_axis).astype(jnp.float32), spread_grad)
    step_grad = split_dot(weighted_grad * conv_in, expand, 1, 2) - decay_grad * prep["rate"]
    step_pre = prep["step_pre"]
    pre_grad = step_grad / (1.0 + jnp.exp(-step_pre))
    step_w_grad_ref[...] += exact_dot(prep["normed"].T, pre_grad)
    normed_grad = (
        exact_dot(pre_grad, step_w, 1, 1)
        + pltpu.roll(b_grad, R, 1)
        + pltpu.roll(c_grad, R + NS, 1)
    )
    unit = prep["unit"]
    rows_grad_ref[0:1, :] += jnp.sum(normed_grad * unit, axis=0, keepdims=True)
    rows_grad_ref[1:2, :] += jnp.sum(pre_grad, axis=0, keepdims=True)
    rows_grad_ref[2:3, :] += jnp.sum(decay_grad * prep["log_decay"], axis=0, keepdims=True)
    unit_grad = normed_grad * prep["gains"]
    along = exact_dot(unit_grad * unit, prep["group_mean"], 1, 1)
    proj_grad_ref[...] = prep["scale"] * (unit_grad - unit * along)


def scan_operands(step_weight, step_bias, log_rate, skip_gain, proj_gains, head_width):
    head_count = step_bias.shape[0]
    channel_count = skip_gain.shape[0]

    def lane_row(values):
        return jnp.pad(values.astype(jnp.float32), (0, LANES - values.shape[0]))[None, :]

    params = jnp.concatenate(
        [
            lane_row(proj_gains),
            lane_row(step_bias),
            lane_row(log_rate),
            jnp.zeros((5, LANES), jnp.float32),
        ],
        axis=0,
    )
    step_w = jnp.pad(
        step_weight.astype(jnp.float32), ((0, LANES - R), (0, LANES - head_count))
    )
    skip = skip_gain.astype(jnp.float32)[None, :]
    owner = lax.broadcasted_iota(jnp.int32, (LANES, channel_count), 1) // head_width
    head = lax.broadcasted_iota(jnp.int32, (LANES, channel_count), 0)
    return params, step_w, skip, (owner == head).astype(jnp.bfloat16)


def whole(shape):
    return pl.BlockSpec(shape, lambda i, *_: (0,) * len(shape))


def scan_forward(bounds, projected, conv_out, gate_pre, operands, head_width):
    params, step_w, skip, expand = operands
    rows, channels = conv_out.shape
    chunks = rows // CHUNK

    def chunk_rows(width):
        return pl.BlockSpec((CHUNK, width), lambda i, *_: (i, 0))

    return pl.pallas_call(
        functools.partial(scan_forward_kernel, head_width),
        out_shape=(
            jax.ShapeDtypeStruct((rows, channels), jnp.bfloat16),
            jax.ShapeDtypeStruct((rows, channels), jnp.float32),
            jax.ShapeDtypeStruct((chunks, NS, channels), jnp.float32),
        ),
        grid_spec=pltpu.PrefetchScalarGridSpec(
            num_scalar_prefetch=1,
            grid=(chunks,),
            in_specs=[
                chunk_rows(LANES),
                chunk_rows(channels),
                chunk_rows(channels),
                whole(params.shape),
                whole(step_w.shape),
                whole(skip.shape),
                whole(expand.shape),
            ],
            out_specs=[
                chunk_rows(channels),
                chunk_rows(channels),
                pl.BlockSpec((1, NS, channels), lambda i, *_: (i, 0, 0)),
            ],
            scratch_shapes=[pltpu.VMEM((NS, channels), jnp.float32)],
        ),
        cost_estimate=pl.CostEstimate(
            flops=100_000_000, bytes_accessed=100_000, transcendentals=0
        ),
        name="scan_forward",
    )(bounds, projected, conv_out, gate_pre, params, step_w, skip, expand)


def scan_backward(bounds, upstream, projected, conv_out, gate_pre, scanned, states, operands, head_width):
    params, step_w, skip, expand = operands
    rows, channels = conv_out.shape
    chunks = rows // CHUNK

    def chunk_rows(width):
        return pl.BlockSpec((CHUNK, width), lambda i, *_: (chunks - 1 - i, 0))

    return pl.pallas_call(
        functools.partial(scan_backward_kernel, head_width),
        out_shape=(
            jax.ShapeDtypeStruct((rows, LANES), jnp.float32),
            jax.ShapeDtypeStruct((rows, channels), jnp.float32),
            jax.ShapeDtypeStruct((rows, channels), jnp.bfloat16),
            jax.ShapeDtypeStruct((LANES, LANES), jnp.float32),
            jax.ShapeDtypeStruct((8, LANES), jnp.float32),
            jax.ShapeDtypeStruct((8, channels), jnp.float32),
        ),
        grid_spec=pltpu.PrefetchScalarGridSpec(
            num_scalar_prefetch=1,
            grid=(chunks,),
            in_specs=[
                chunk_rows(channels),
                chunk_rows(LANES),
                chunk_rows(channels),
                chunk_rows(channels),
                chunk_rows(channels),
                pl.BlockSpec((1, NS, channels), lambda i, *_: (chunks - 1 - i, 0, 0)),
                whole(params.shape),
                whole(step_w.shape),
                whole(skip.shape),
                whole(expand.shape),
            ],
            out_specs=[
                chunk_rows(LANES),
                chunk_rows(channels),
                chunk_rows(channels),
                whole((LANES, LANES)),
                whole((8, LANES)),
                whole((8, channels)),
            ],
            scratch_shapes=[pltpu.VMEM((NS, channels), jnp.float32)],
        ),
        cost_estimate=pl.CostEstimate(
            flops=100_000_000, bytes_accessed=100_000, transcendentals=0
        ),
        name="scan_backward",
    )(bounds, upstream, projected, conv_out, gate_pre, scanned, states, params, step_w, skip, expand)


PLACES = (0, 2, 1, 3)


def swap_pairs(size, flip):
    return [(index, index ^ flip) for index in range(size)]


class Wires:
    def __init__(self, dp_size, tensor_size):
        self.dp_size = dp_size
        self.tensor_size = tensor_size
        self.staged = tensor_size == 4 and dp_size == 8
        self.group = lax.axis_index("dp")
        self.lane = lax.axis_index("tensor")
        self.outer = self.group // 2
        self.inner = self.group % 2
        self.turn = jnp.bitwise_xor(self.lane, self.outer)

    def over_tensor(self, values, flip):
        return lax.ppermute(values, "tensor", swap_pairs(self.tensor_size, flip))

    def over_dp(self, values, flip):
        return lax.ppermute(values, "dp", swap_pairs(self.dp_size, flip))

    def place_of(self, distance):
        block = jnp.bitwise_xor(self.turn, distance)
        return (block & 1) * 2 + (block >> 1)


    def gather_features(self, values, until=None, deadline=None):
        if not self.staged:
            rows = lax.all_gather(values, "tensor", axis=1, tiled=True)
            return rows if deadline is None else (rows, deadline)
        across = self.over_tensor(values, 2)
        beside = self.over_tensor(values, 1)
        diagonal = self.over_tensor(across if until is None else after(across, until), 1)
        if deadline is not None:
            across, beside, diagonal, deadline = lax.optimization_barrier(
                (across, beside, diagonal, deadline)
            )
        rows = jnp.concatenate([values, across, beside, diagonal], axis=1)
        return rows if deadline is None else (rows, deadline)

    def sum_features(self, project, start=None, until=None, across_start=None):
        width = D // self.tensor_size
        if not self.staged:
            return lax.psum_scatter(
                project(slice(0, D)), "tensor", scatter_dimension=1, tiled=True
            )
        sent = project(slice(2 * width, 4 * width)).astype(jnp.bfloat16)
        if start is not None:
            sent = after(sent, start)
        kept = project(slice(0, 2 * width))
        total = kept + self.over_tensor(sent, 1).astype(jnp.float32)
        passed = total[:, width:].astype(jnp.bfloat16)
        if across_start is not None:
            passed = after(passed, across_start)
        across = self.over_tensor(passed, 2)
        if until is not None:
            across = after(across, until)
        return total[:, :width] + across.astype(jnp.float32)

    def sum_small(self, values):
        if not self.staged:
            return lax.psum(values, "tensor")
        values = values + self.over_tensor(values, 1)
        return values + self.over_tensor(values, 2)

    def sum_rows(self, values, wire):
        if not self.staged:
            return lax.psum(values.astype(wire), "tensor").astype(jnp.float32)
        half = values.shape[0] // 2
        core = self.lane % 2
        kept = lax.dynamic_slice_in_dim(values, core * half, half)
        sent = lax.dynamic_slice_in_dim(values, (1 - core) * half, half)
        total = kept + self.over_tensor(sent.astype(wire), 1).astype(jnp.float32)
        total = total + self.over_tensor(total.astype(wire), 2).astype(jnp.float32)
        other = self.over_tensor(total.astype(wire), 1).astype(jnp.float32)
        total = total.astype(wire).astype(jnp.float32)
        first = jnp.where(core == 0, total, other)
        second = jnp.where(core == 0, other, total)
        return jnp.concatenate([first, second], axis=0)


    def block_order(self):
        return jnp.stack([jnp.bitwise_xor(self.lane, place) for place in PLACES]).astype(jnp.int32)

    def gather_whole(self, shard, widths):
        whole_rows = lax.all_gather(shard, "dp", axis=0, tiled=True)
        if not self.staged:
            return split_columns(whole_rows, widths)
        return move_blocks(self.block_order(), whole_rows, widths)

    def sum_whole(self, grads, earlier=None):
        widths = [grad.shape[1] for grad in grads]
        if self.staged:
            joined = restore_blocks(self.block_order(), grads)
        else:
            joined = jnp.concatenate(grads, axis=1)
        if earlier is not None:
            joined = after(joined, earlier)
        total = lax.psum_scatter(joined, "dp", scatter_dimension=0, tiled=True)
        return [part.astype(jnp.float32) for part in split_columns(total, widths)], joined


    def sum_across(self, grad):
        blocks = grad.reshape(4, 2, D // 8, grad.shape[1])
        sent = lax.dynamic_index_in_dim(blocks, 1 - self.inner, 1, keepdims=False)
        kept = lax.dynamic_index_in_dim(blocks, self.inner, 1, keepdims=False)
        return kept, self.over_dp(sent, 1)

    def sum_far(self, across, marker):
        kept, got = across
        total = (kept.astype(jnp.float32) + after(got, marker).astype(jnp.float32)).astype(
            jnp.bfloat16
        )

        def pair(near, far):
            return [
                lax.dynamic_index_in_dim(total, self.place_of(place), 0, keepdims=False)
                for place in (near, far)
            ]

        return pair(0, 1), self.over_dp(jnp.concatenate(pair(2, 3), axis=0), 4)

    def sum_near(self, far, marker):
        (own, near), got = far
        got = after(got, marker).astype(jnp.float32)
        rows = own.shape[0]
        sent = (near.astype(jnp.float32) + got[rows:]).astype(jnp.bfloat16)
        return own.astype(jnp.float32) + got[:rows], self.over_dp(sent, 2)

    def sum_end(self, near):
        total, got = near
        return total + got.astype(jnp.float32)

    def exchange(self, blocks):
        return lax.all_to_all(blocks, "dp", split_axis=0, concat_axis=0, tiled=True)


def split_columns(values, widths):
    parts, start = [], 0
    for width in widths:
        parts.append(values[:, start : start + width])
        start += width
    return parts


def move_kernel(order_ref, whole_ref, *outs):
    start = 0
    for out in outs:
        width = out.shape[1]
        out[...] = whole_ref[:, start : start + width]
        start += width


def move_blocks(order, gathered, widths):
    rows, width = gathered.shape
    block = rows // 4
    return pl.pallas_call(
        move_kernel,
        out_shape=[jax.ShapeDtypeStruct((rows, part), jnp.bfloat16) for part in widths],
        grid_spec=pltpu.PrefetchScalarGridSpec(
            num_scalar_prefetch=1,
            grid=(4,),
            in_specs=[pl.BlockSpec((block, width), lambda i, order_ref: (order_ref[i], 0))],
            out_specs=[
                pl.BlockSpec((block, part), lambda i, order_ref: (i, 0)) for part in widths
            ],
        ),
        cost_estimate=pl.CostEstimate(
            flops=0, bytes_accessed=4 * rows * width, transcendentals=0
        ),
        name="move_blocks",
    )(order, gathered)


def restore_kernel(order_ref, *refs):
    out, start = refs[-1], 0
    for ref in refs[:-1]:
        width = ref.shape[1]
        out[:, start : start + width] = ref[...]
        start += width


def restore_blocks(order, grads):
    rows = grads[0].shape[0]
    block = rows // 4
    width = sum(grad.shape[1] for grad in grads)
    return pl.pallas_call(
        restore_kernel,
        out_shape=jax.ShapeDtypeStruct((rows, width), jnp.bfloat16),
        grid_spec=pltpu.PrefetchScalarGridSpec(
            num_scalar_prefetch=1,
            grid=(4,),
            in_specs=[
                pl.BlockSpec((block, grad.shape[1]), lambda i, order_ref: (i, 0))
                for grad in grads
            ],
            out_specs=pl.BlockSpec((block, width), lambda i, order_ref: (order_ref[i], 0)),
        ),
        cost_estimate=pl.CostEstimate(
            flops=0, bytes_accessed=4 * rows * width, transcendentals=0
        ),
        name="restore_blocks",
    )(order, *grads)


def pack_rows(parts, lanes):
    blocks = parts[0].shape[0]
    flat = jnp.concatenate([part.reshape(blocks, -1) for part in parts], axis=1)
    size = flat.shape[1]
    rows = -(-size // (16 * lanes)) * 16
    flat = jnp.pad(flat, ((0, 0), (0, rows * lanes - size)))
    return flat.reshape(blocks, rows, lanes)


def unpack_rows(packed, shapes):
    blocks = packed.shape[0]
    flat = packed.reshape(blocks, -1)
    parts, start = [], 0
    for shape in shapes:
        size = 1
        for extent in shape:
            size *= extent
        parts.append(flat[:, start : start + size].reshape((blocks,) + shape))
        start += size
    return parts


def after(values, earlier):
    return lax.optimization_barrier((values, earlier))[0]


def row_scale(wires, values):
    mean_square = wires.sum_small(jnp.sum(values * values, axis=1).reshape(-1, LANES)) / D
    return lax.rsqrt(mean_square + EPSILON).reshape(-1)


def norm_back(wires, values, inverse, gain, upstream):
    normed = values * inverse[:, None]
    gain_grad = jnp.sum(upstream * normed, axis=0)
    scaled = upstream * gain
    along = jnp.sum(scaled * normed, axis=1).reshape(-1, LANES)
    along = wires.sum_small(along).reshape(-1) / D
    return inverse[:, None] * (scaled - normed * along[:, None]), gain_grad


def per_device(
    dp_size,
    tensor_size,
    tokens,
    out_grad,
    lengths,
    deal,
    mixer_gain,
    inner_weight,
    gate_weight,
    conv_taps,
    conv_bias,
    proj_weight,
    proj_gains,
    step_weight,
    step_bias,
    log_rate,
    skip_gain,
    out_weight,
    ffn_gain,
    ffn_gate,
    ffn_up,
    ffn_down,
):
    wires = Wires(dp_size, tensor_size)
    group = wires.group
    bf16, f32 = jnp.bfloat16, jnp.float32

    packed_lengths = lengths[deal]
    group_lengths = lax.dynamic_slice_in_dim(packed_lengths, group * SPG, SPG)
    starts = jnp.cumsum(group_lengths) - group_lengths
    filled = jnp.sum(group_lengths)
    bounds = jnp.concatenate([starts[1:], filled[None]]).astype(jnp.int32)
    row_ids = jnp.arange(GCAP, dtype=jnp.int32)
    live_rows = row_ids < filled
    segment = jnp.sum((row_ids[:, None] >= bounds[None, :]).astype(jnp.int32), axis=1)
    slot = jnp.minimum(segment, SPG - 1)
    position = row_ids - jnp.where(slot == 0, 0, starts[slot])
    span = LMAX // dp_size

    small_parts = (
        proj_weight,
        mixer_gain,
        conv_taps,
        conv_bias,
        proj_gains,
        step_weight,
        step_bias,
        log_rate,
        skip_gain,
        ffn_gain,
    )
    small_shapes = [part.shape for part in small_parts]
    small = pack_rows([part[None] for part in small_parts], tokens.shape[2])
    small_rows = small.shape[1]
    order = jnp.arange(dp_size, dtype=jnp.int32)
    if wires.staged:
        order = jnp.bitwise_xor(order, group)
    dealt = tokens[deal.reshape(dp_size, SPG)[order].reshape(-1)].reshape(dp_size, SPG * span, -1)
    sent = jnp.concatenate([dealt, jnp.broadcast_to(small, (dp_size,) + small.shape[1:])], axis=1)
    if wires.staged:
        arrived = jnp.stack(
            [sent[0]] + [wires.over_dp(sent[flip], flip) for flip in range(1, dp_size)]
        )
    else:
        arrived = wires.exchange(sent)
    flat_rows = arrived.reshape(dp_size * (SPG * span + small_rows), -1)
    origin = position // span
    if wires.staged:
        origin = jnp.bitwise_xor(origin, group)
    source_rows = origin * (SPG * span + small_rows) + slot * span + position % span
    source_rows = jnp.where(live_rows, source_rows, 0)
    packed = jnp.where(live_rows[:, None], flat_rows[source_rows], 0.0).astype(f32)
    small = unpack_rows(arrived[:, SPG * span :][order], small_shapes)

    def along_last(part):
        return jnp.moveaxis(part, 0, -2).reshape(part.shape[1:-1] + (-1,))

    proj_all = small[0].reshape(-1, small[0].shape[-1])
    gain_all, taps_all, bias_all, gains_all, step_w_all, step_b_all, rate_all, skip_all, ffn_gain_all = [
        along_last(part).astype(f32) for part in small[1:]
    ]

    staged = wires.staged
    in_width, out_width = [inner_weight.shape[1]], [out_weight.shape[0]]
    down_width, ffn_widths = [ffn_down.shape[0]], [ffn_gate.shape[1], ffn_up.shape[1]]
    inner_all, gate_all, out_all = wires.gather_whole(
        jnp.concatenate([inner_weight, gate_weight, out_weight.T], axis=1), in_width * 2 + out_width
    )

    inverse_in = row_scale(wires, packed)
    mixer_rows = wires.gather_features((packed * inverse_in[:, None] * gain_all).astype(bf16))
    ffn_gate_all, ffn_up_all, ffn_down_all = wires.gather_whole(
        after(jnp.concatenate([ffn_gate, ffn_up, ffn_down.T], axis=1), (inner_all, mixer_rows)),
        ffn_widths + down_width,
    )
    inner_pre = contract(mixer_rows, inner_all, 1, 0)
    conv_out = conv_silu(inner_pre, taps_all, bias_all, segment).astype(bf16)
    proj_terms = contract(conv_out, proj_all, 1, 0)
    projected = wires.sum_rows(proj_terms, f32)
    gate_pre = contract(mixer_rows, gate_all, 1, 0)
    operands = scan_operands(step_w_all, step_b_all, rate_all, skip_all, gains_all, HEAD_WIDTH)
    out_cot = jnp.where(live_rows[:, None], out_grad, 0.0).astype(bf16)
    gated, scanned, states = scan_forward(
        bounds, projected, conv_out, gate_pre, operands, HEAD_WIDTH
    )
    cot_rows, gated = wires.gather_features(after(out_cot, proj_terms), deadline=gated)
    residual = packed + wires.sum_features(lambda rows: contract(gated, out_all[rows], 1, 1))

    inverse_mid = row_scale(wires, residual)
    ffn_rows = wires.gather_features((residual * inverse_mid[:, None] * ffn_gain_all).astype(bf16), ffn_gate_all)
    gate_ffn = contract(ffn_rows, ffn_gate_all, 1, 0)
    up_ffn = contract(ffn_rows, ffn_up_all, 1, 0)
    logistic = jax.nn.sigmoid(gate_ffn)
    activated = gate_ffn * logistic
    hidden = (activated * up_ffn).astype(bf16)

    hidden_grad = contract(cot_rows, ffn_down_all, 1, 0)
    gate_grad = (hidden_grad * up_ffn * logistic * (1.0 + gate_ffn * (1.0 - logistic))).astype(bf16)
    up_grad = (hidden_grad * activated).astype(bf16)
    ffn_gate_terms = contract(ffn_rows, gate_grad, 0, 0).astype(bf16)
    ffn_up_terms = contract(ffn_rows, up_grad, 0, 0).astype(bf16)
    down_terms = contract(cot_rows, hidden, 0, 0).astype(bf16)
    (ffn_down_grad, ffn_gate_grad, ffn_up_grad), sums_ready = wires.sum_whole(
        [down_terms, ffn_gate_terms, ffn_up_terms]
    )
    mid_grad = wires.sum_features(
        lambda rows: contract(gate_grad, ffn_gate_all[rows], 1, 1)
        + contract(up_grad, ffn_up_all[rows], 1, 1),
        until=sums_ready,
    )
    mid_back, ffn_gain_grad = norm_back(wires, residual, inverse_mid, ffn_gain_all, mid_grad)
    residual_grad = out_cot.astype(f32) + mid_back
    branch = residual_grad.astype(bf16)
    branch_rows = wires.gather_features(branch)
    gated_grad = contract(branch_rows, out_all, 1, 0)
    final_rows = residual + wires.sum_features(
        lambda rows: contract(hidden, ffn_down_all[rows], 1, 1), start=branch_rows
    )
    out_terms = contract(branch_rows, gated, 0, 0).astype(bf16)
    proj_part, conv_core_grad, gate_low, step_w_part, row_parts, skip_part = scan_backward(
        bounds, gated_grad, projected, conv_out, gate_pre, scanned, states, operands, HEAD_WIDTH
    )
    gate_terms = contract(after(mixer_rows, proj_part), gate_low, 0, 0).astype(bf16)
    if staged:
        proj_part, final_rows = lax.optimization_barrier((proj_part, final_rows))
    output = jnp.where(live_rows[:, None], final_rows, 0.0).astype(bf16)
    head_count = step_b_all.shape[0]
    gains_grad = wires.sum_small(row_parts)[0]
    proj_low = wires.sum_rows(proj_part, bf16).astype(bf16)
    conv_grad = conv_core_grad + contract(proj_low, proj_all, 1, 1)
    proj_weight_grad = contract(conv_out, proj_low, 0, 0)

    def conv_piece(inner_in, taps_in, bias_in):
        return conv_silu(inner_in, taps_in, bias_in, segment)

    unused_conv, conv_pull = jax.vjp(conv_piece, inner_pre, taps_all, bias_all)
    inner_grad, taps_grad, bias_grad = conv_pull(conv_grad)
    inner_low = inner_grad.astype(bf16)
    inner_terms = contract(mixer_rows, inner_low, 0, 0).astype(bf16)
    (inner_weight_grad, gate_weight_grad, out_weight_grad), last_joined = wires.sum_whole(
        [inner_terms, gate_terms, out_terms], ffn_gate_grad
    )
    in_grad = wires.sum_features(
        lambda rows: contract(inner_low, inner_all[rows], 1, 1)
        + contract(gate_low, gate_all[rows], 1, 1),
        until=inner_terms,
    )
    in_back, mixer_gain_grad = norm_back(wires, packed, inverse_in, gain_all, in_grad)

    def by_index(part):
        split = part.reshape(part.shape[:-1] + (dp_size, part.shape[-1] // dp_size))
        return jnp.moveaxis(split, -2, 0)

    small_grads = pack_rows(
        [
            part.astype(bf16)
            for part in (
                proj_weight_grad.reshape(dp_size, -1, proj_weight_grad.shape[1]),
                by_index(mixer_gain_grad),
                by_index(taps_grad),
                by_index(bias_grad),
                by_index(gains_grad),
                by_index(step_w_part[:R, :head_count]),
                by_index(row_parts[1, :head_count]),
                by_index(row_parts[2, :head_count]),
                by_index(skip_part[0]),
                by_index(ffn_gain_grad),
            )
        ],
        tokens.shape[2],
    )

    grad_packed = (residual_grad + in_back).astype(bf16)
    slot_position = jnp.arange(LMAX, dtype=jnp.int32).reshape(dp_size, 1, span)
    slot_live = slot_position < group_lengths[None, :, None]
    slot_rows = jnp.where(slot_live, starts[None, :, None] + slot_position, 0).reshape(-1)
    leaving = jnp.where(slot_live.reshape(-1)[:, None], grad_packed[slot_rows], 0.0)
    leaving = leaving.reshape(dp_size, SPG * span, -1)
    returned = wires.exchange(jnp.concatenate([leaving, small_grads], axis=1))
    inverse_deal = jnp.zeros_like(deal).at[deal].set(
        jnp.arange(deal.shape[0], dtype=jnp.int32)
    )
    tokens_grad = returned[:, : SPG * span].reshape(dp_size * SPG, span, -1)[inverse_deal]
    (
        proj_weight_grad,
        mixer_gain_grad,
        taps_grad,
        bias_grad,
        gains_grad,
        step_w_grad,
        step_b_grad,
        rate_grad,
        skip_grad,
        ffn_gain_grad,
    ) = unpack_rows(
        jnp.sum(returned[:, SPG * span :].astype(f32), axis=0)[None], small_shapes
    )

    return (
        output,
        tokens_grad,
        mixer_gain_grad[0],
        inner_weight_grad,
        gate_weight_grad,
        taps_grad[0],
        bias_grad[0],
        proj_weight_grad[0],
        gains_grad[0],
        step_w_grad[0],
        step_b_grad[0],
        rate_grad[0],
        skip_grad[0],
        out_weight_grad.T,
        ffn_gain_grad[0],
        ffn_gate_grad,
        ffn_up_grad,
        ffn_down_grad.T,
    )


def solution(mesh):
    return jax.shard_map(
        functools.partial(per_device, mesh.shape["dp"], mesh.shape["tensor"]),
        mesh=mesh,
        in_specs=(
            P(None, "dp", "tensor"),
            P("dp", "tensor"),
            P(),
            P(),
            P(("tensor", "dp")),
            P("dp", "tensor"),
            P("dp", "tensor"),
            P(None, ("tensor", "dp")),
            P(("tensor", "dp")),
            P(("tensor", "dp"), None),
            P("dp"),
            P(None, ("tensor", "dp")),
            P(("tensor", "dp")),
            P(("tensor", "dp")),
            P(("tensor", "dp")),
            P("tensor", "dp"),
            P(("tensor", "dp")),
            P("dp", "tensor"),
            P("dp", "tensor"),
            P("tensor", "dp"),
        ),
        out_specs=(
            P("dp", "tensor"),
            P(None, "dp", "tensor"),
            P(("tensor", "dp")),
            P("dp", "tensor"),
            P("dp", "tensor"),
            P(None, ("tensor", "dp")),
            P(("tensor", "dp")),
            P(("tensor", "dp"), None),
            P("dp"),
            P(None, ("tensor", "dp")),
            P(("tensor", "dp")),
            P(("tensor", "dp")),
            P(("tensor", "dp")),
            P("tensor", "dp"),
            P(("tensor", "dp")),
            P("dp", "tensor"),
            P("dp", "tensor"),
            P("tensor", "dp"),
        ),
        check_vma=False,
    )
```
